32 devices in a mesh: groups: 2 (over y), dp: 4 (over z), tensor: 4 (over x, core).
Axes of the slice: x: 2, y: 2, z: 4, core: 2. Of those that a mesh axis runs over, the one named last changes fastest.
Arguments:
- feature_cache: bfloat16 [512, 8, 3, 8192], P(('groups', 'dp'), None, None, 'tensor'), parts along dimension 0
- owner_ids: int32 [512, 1], P(('groups', 'dp')), parts along dimension 0, may hold values from 0 to 3; in each aligned block of 64 rows (0 to 63, 64 to 127, ...) at most 24 rows name the same one
- slot_ids: int32 [512], P(('groups', 'dp')), parts along dimension 0, may hold values from 0 to 63
- live_tokens: int32 [512], P(('groups', 'dp')), parts along dimension 0, may hold values from 1 to 8
- tap_gain: float32 [3, 8192], P(None, 'tensor'), may hold values from 0.1 to 1.9
- key_cotangent: bfloat16 [4096, 1024], P(('groups', 'dp'), 'tensor'), parts along dimension 0, may hold values from -0.1875 to 0.1875
- value_cotangent: bfloat16 [4096, 1024], P(('groups', 'dp'), 'tensor'), parts along dimension 0, may hold values from -0.1875 to 0.1875
Outputs:
- kv_gradient: float32 [4096, 8192], P(('groups', 'dp'), 'tensor'), parts along dimension 0
The draws below stay inside these ranges and needn't reach their ends.
There are 2 independent parts, one for each index of `groups`. The reference program is written for one: setup_inputs(seed, part) draws one part's arguments, and reference() takes and returns one part's arrays. A program takes and returns all parts, laid end to end along the dimension named above; an argument that names none is the same for every part. Nothing has to cross between parts.
Inputs may be any that keep to these rules, and one draw needn't show every extreme that they name: `owner_ids`: among the 64 entries of one device's list, no owner is named more than 24 times, a bound that some block reaches.
All inputs are finite; a program needn't handle non-finite values.
Results may differ from the reference program's by a relative error of at most 0.009.
Values may be sent and summed in bfloat16 or wider, within the bound.
A program may use at most 128 MiB of HBM per device.

```python
import math
import jax
import jax.numpy as jnp
import numpy as np
from jax import lax

D = 8192
KV_HEADS = 8
HEAD = 128
TAPS = 3
BLOCK = 8
TOK_DEV = 512
FETCH = 64
CAP = 24
BLOCKS = 256
TOKENS = 2048
N_DP = 4


def draw_feature_cache(key, part):
    key_noise, key_column, key_row = jax.random.split(key, 3)
    full_shape = (BLOCKS, BLOCK, TAPS, D)
    column = jnp.arange(D, dtype=jnp.float32) / D
    noise = jax.random.normal(key_noise, full_shape, jnp.float32)
    column_scale = 10.0 ** column * jax.random.uniform(key_column, (D,), jnp.float32, 0.7, 1.3)
    row_scale = 10.0 ** jax.random.uniform(key_row, (BLOCKS, BLOCK, TAPS, 1), jnp.float32, 0.0, 1.0)
    return (noise * column_scale * row_scale).astype(jnp.bfloat16)


def touch_ends(values, rng, least, largest):
    longest = values.shape.index(max(values.shape))
    spots = []
    for shift in (0, 1):
        where = [jax.random.randint(jax.random.fold_in(rng, axis), (), 0, length) for axis, length in enumerate(values.shape)]
        where[longest] = (where[longest] + shift) % values.shape[longest]
        spots.append(tuple(where))
    return values.at[spots[0]].set(least).at[spots[1]].set(largest)


def spiked(drawn, key, source, target, shards_of, factor):
    def block_of(axis_at):
        return (jnp.arange(drawn.shape[axis_at]) // (drawn.shape[axis_at] // shards_of)).reshape((-1,) + (1,) * (drawn.ndim - 1 - axis_at))

    one_side = jax.random.permutation(key, shards_of)[block_of(target)]
    second = (block_of(target) + shards_of // 2) % shards_of
    return jnp.where((block_of(source) == one_side) | (block_of(source) == second), factor * drawn, drawn)


def steps_of(rng, shape, cuts, low, high):
    loudness, own = 1.0, jax.random.fold_in(rng, 6)
    for axis_at, blocks in cuts:
        heights = jnp.exp(jax.random.uniform(jax.random.fold_in(own, axis_at), (blocks,), jnp.float32, low / len(cuts), high / len(cuts)))
        loudness = loudness * jnp.repeat(heights, shape[axis_at] // blocks).reshape([-1 if axis == axis_at else 1 for axis in range(len(shape))])
    return loudness


def deal_out(stream_key, own, number, rows, count, top, bound, skew):
    order = jax.random.permutation(stream_key, count)
    heavy_load, common = portions_of(count, rows * top, bound, skew, True), portions_of(count, rows * top, bound, skew, False)
    places = jnp.arange(count)

    def named(tallies, turn):
        used = int((tallies > 0).sum())
        fixed = max(1, used // 4)
        passed = fixed + (places - fixed + turn * (used - fixed)) % max(1, count - fixed)
        return jnp.zeros((count,), jnp.int32).at[order[jnp.where(places < fixed, places, passed)]].set(jnp.asarray(tallies, jnp.int32))

    tallies = jnp.where(number % 4 == 0, named(heavy_load, number // 4), named(common, number - number // 4 - 1))
    mixed = jax.random.permutation(jax.random.fold_in(own, 3), count)
    source_of, sink = mixed[0:count // 2 * 2:2], mixed[1:count // 2 * 2:2]
    margin = jnp.minimum(tallies[source_of] - 1, bound - tallies[sink]) // 2
    margin = jnp.where((source_of == order[0]) | (sink == order[0]) | (tallies[sink] == 0), 0, jnp.maximum(margin, 0))
    passed = jax.random.randint(jax.random.fold_in(own, 4), (count // 2,), 0, 1 << 20) % (margin + 1)
    tallies = tallies.at[source_of].add(-passed).at[sink].add(passed)
    items = jnp.searchsorted(jnp.cumsum(tallies), jnp.arange(rows * top), side="right").astype(jnp.int32)
    listing = items.reshape(top, rows).T
    listing = listing[jax.random.permutation(jax.random.fold_in(own, 1), rows)]
    turn = jax.random.randint(jax.random.fold_in(own, 2), (rows, 1), 0, top)
    return jnp.take_along_axis(listing, (jnp.arange(top)[None, :] + turn) % top, axis=1)


def portions_of(amount, total, limit, skew, full):
    weights = [(1 << 20) // math.isqrt(rank ** skew) + 1 for rank in range(1, amount + 1)]
    largest = limit if full else min(limit, max(-(-total // amount), total * weights[0] // sum(weights)))
    least = 1 if total - largest >= amount - 1 else 0
    holding, spare = [largest] + [least] * (amount - 1), total - largest - least * (amount - 1)
    while spare > 0:
        free = [i for i in range(1, amount) if holding[i] < largest] or [i for i in range(1, amount) if holding[i] < limit]
        pool, budget = sum([weights[i] for i in free]), spare
        for i in free:
            addition = min(limit - holding[i], max(1, budget * weights[i] // pool), spare)
            holding[i] = holding[i] + addition
            spare = spare - addition
    return np.array(holding)


def noise_with(rng, dims, width, most, cuts, heavy, kind=jnp.bfloat16):
    drawn = width * jax.random.normal(rng, dims, jnp.float32)
    if cuts:
        drawn = drawn * steps_of(rng, dims, cuts, -0.22, 0.18)
    return jnp.clip(spiked(drawn, jax.random.fold_in(rng, 3), *heavy), -most, most).astype(kind)


def setup_inputs(seed: int = 0, part: int = 0) -> dict:
    splits = jax.random.split(jax.random.key(seed), 8)
    own_keys = jax.random.split(jax.random.fold_in(splits[7], part), 8)
    feature_cache = draw_feature_cache(jax.random.fold_in(jax.random.fold_in(splits[7], part), 71), part)
    owner_ids_keys = jax.random.split(jax.random.fold_in(own_keys[1], 1), BLOCKS // FETCH)
    owner_ids_turns = jax.random.permutation(jax.random.fold_in(own_keys[1], 3), BLOCKS // FETCH)
    owner_ids = jax.vmap(lambda own, number: deal_out(jax.random.fold_in(own_keys[1], 2), own, number, FETCH, N_DP, 1, CAP, 2))(owner_ids_keys, owner_ids_turns).reshape((BLOCKS, 1))
    slot_ids = touch_ends(jax.random.randint(own_keys[2], (BLOCKS,), 0, FETCH), jax.random.fold_in(own_keys[2], 1), 0, FETCH - 1).astype(jnp.int32)
    live_tokens = touch_ends(jax.random.randint(own_keys[3], (BLOCKS,), 1, BLOCK + 1), jax.random.fold_in(own_keys[3], 1), 1, BLOCK).astype(jnp.int32)
    tap_gain = jnp.clip(1.0 + 0.18 * jax.random.normal(splits[4], (TAPS, D), jnp.float32), 0.1, 1.9)
    key_cotangent = noise_with(own_keys[5], (TOKENS, KV_HEADS * HEAD), TOKENS ** -0.5, 0.1875, ((0, 4), (1, 4)), (0, 1, 4, 2.0))
    value_cotangent = noise_with(own_keys[6], (TOKENS, KV_HEADS * HEAD), TOKENS ** -0.5, 0.1875, ((0, 4), (1, 4)), (0, 1, 4, 2.0))
    return dict(feature_cache=feature_cache, owner_ids=owner_ids, slot_ids=slot_ids, live_tokens=live_tokens, tap_gain=tap_gain, key_cotangent=key_cotangent, value_cotangent=value_cotangent)


epsilon = 1e-06

def reference(feature_cache, owner_ids, slot_ids, live_tokens, tap_gain, key_cotangent, value_cotangent):
    block_index = (owner_ids[:, 0] * FETCH + slot_ids).astype(jnp.int32)
    cotangent = jnp.concatenate([key_cotangent, value_cotangent], axis=1)
    offsets = jnp.arange(BLOCK, dtype=jnp.int32)

    def add_shard(accumulated, step_index):
        first_block = (step_index * FETCH).astype(jnp.int32)
        chosen_ids = lax.dynamic_slice_in_dim(block_index, first_block, FETCH, 0)
        live_counts = lax.dynamic_slice_in_dim(live_tokens, first_block, FETCH, 0)
        floats = jnp.take(feature_cache, chosen_ids, axis=0).astype(jnp.float32)
        mean_square = lax.optimization_barrier(jnp.mean(floats * floats, axis=-1, keepdims=True))
        normed = floats * lax.rsqrt(mean_square + epsilon) * tap_gain
        live_mask = (offsets[None, :] < live_counts[:, None]).astype(jnp.float32)
        united = (lax.optimization_barrier(jnp.sum(normed, axis=2)) * live_mask[:, :, None]).astype(jnp.bfloat16).reshape(TOK_DEV, D)
        first_row = (step_index * TOK_DEV).astype(jnp.int32)
        grads = lax.dynamic_slice_in_dim(cotangent, first_row, TOK_DEV, 0)
        partial_value = lax.dot_general(grads, united, (((0,), (0,)), ((), ())), preferred_element_type=jnp.float32)
        partial_value = lax.optimization_barrier(partial_value.astype(jnp.bfloat16)).astype(jnp.float32)
        return (accumulated + partial_value, None)
    start_value = jnp.zeros((cotangent.shape[1], D), jnp.float32)
    kv_gradient, _ = lax.scan(add_shard, start_value, jnp.arange(N_DP, dtype=jnp.int32))
    return kv_gradient
```

```python
import functools

import jax
import jax.numpy as jnp
from jax import lax
from jax.experimental import pallas as pl
from jax.experimental.pallas import tpu as pltpu
from jax.sharding import PartitionSpec as P

EPSILON = 1e-06
MESH = pl.DeviceIdType.MESH
LANES = 128


def united_of(feature_cache, tap_gain, width):
    floats = feature_cache.astype(jnp.float32)
    squares = lax.psum(jnp.sum(floats * floats, axis=-1), "tensor")
    inverse_rms = lax.rsqrt(squares / width + EPSILON)
    return jnp.sum(floats * inverse_rms[..., None] * tap_gain, axis=2).astype(jnp.bfloat16)


def slot_matrix(owner_ids, slot_ids, live_tokens, owned, dtype):
    index = owner_ids[:, 0] * owned + slot_ids
    table = lax.all_gather(jnp.stack([index, live_tokens]), "dp", axis=1, tiled=True)
    slots = lax.axis_size("dp") * owned
    chosen = jnp.arange(slots, dtype=jnp.int32)[:, None] == table[0][None, :]
    return chosen.astype(dtype), table[1]


def gather_body(feature_cache, owner_ids, slot_ids, live_tokens, tap_gain, key_cotangent, value_cotangent):
    owned, block_len, _, columns = feature_cache.shape
    width = columns * lax.axis_size("tensor")
    united = united_of(feature_cache, tap_gain, width).reshape(owned * block_len, columns)
    everywhere = lax.all_gather(united, "dp", axis=0, tiled=True)
    chosen, live = slot_matrix(owner_ids, slot_ids, live_tokens, owned, jnp.bfloat16)
    joined = jnp.concatenate(
        [
            lax.all_gather(key_cotangent, "tensor", axis=1, tiled=True),
            lax.all_gather(value_cotangent, "tensor", axis=1, tiled=True),
        ],
        axis=1,
    )
    mine = lax.all_to_all(joined, "dp", split_axis=1, concat_axis=0, tiled=True)
    rows = mine.shape[1]
    mine = mine.reshape(-1, block_len, rows)
    mask = jnp.arange(block_len, dtype=jnp.int32)[None, :] < live[:, None]
    mine = jnp.where(mask[:, :, None], mine, jnp.zeros_like(mine)).reshape(-1, block_len * rows)
    by_slot = lax.dot_general(
        chosen, mine, (((1,), (0,)), ((), ())), preferred_element_type=jnp.float32
    ).astype(jnp.bfloat16).reshape(-1, rows)
    return lax.dot_general(
        by_slot, everywhere, (((0,), (0,)), ((), ())), preferred_element_type=jnp.float32
    )


def line_kernel(
    feats, tab, gain, key, value, out,
    xbuf, psq, sums, invb, united, given, tabs, slots, cbuf,
    xsem, bsend, brecv, gsend, grecv, ssend, srecv, usend, urecv, asend, arecv, csend, crecv,
):
    g, z, t = (lax.axis_index(n) for n in ("groups", "dp", "tensor"))
    owned, taps, block, columns = feats.shape
    tokens = owned * block
    part = key.shape[1]
    chunks = columns // LANES
    half = 2 * part
    width = columns * 4
    inner = jnp.logical_or(z == 1, z == 2)
    outer = jnp.logical_not(inner)
    partner = 3 - z
    near = jnp.where(z < 2, 1, 2)
    far = 3 - near
    edge = jnp.where(z == 1, 0, 3)

    groups_of = 4
    per = owned // groups_of

    def fetch(i):
        return pltpu.make_async_copy(feats.at[pl.ds(i * per, per)], xbuf.at[pl.ds(i * per, per)], xsem.at[i])

    for i in range(groups_of):
        fetch(i).start()

    barrier = pltpu.get_barrier_semaphore()
    for k in range(1, 4):
        pl.semaphore_signal(barrier, inc=1, device_id=(g, lax.rem(z + k, 4), t), device_id_type=MESH)
        pl.semaphore_signal(barrier, inc=1, device_id=(g, z, lax.rem(t + k, 4)), device_id_type=MESH)
    pl.semaphore_wait(barrier, 6)

    def table_to(i):
        return pltpu.make_async_remote_copy(
            tab, tabs.at[z], bsend.at[i - 1], brecv.at[z], device_id=(g, i, t), device_id_type=MESH)

    def table_from(k):
        return pltpu.make_async_remote_copy(
            tab, tabs.at[k], bsend.at[0], brecv.at[k], device_id=(g, near, t), device_id_type=MESH)

    def heads_to(i):
        return pltpu.make_async_remote_copy(
            key if i == 1 else value, given.at[pl.ds(z * tokens, tokens)], gsend.at[i - 1], grecv.at[z],
            device_id=(g, i, t), device_id_type=MESH)

    def heads_own(i):
        return pltpu.make_async_copy(
            key if i == 1 else value, given.at[pl.ds(i * tokens, tokens)], gsend.at[2])

    def heads_from(k):
        return pltpu.make_async_remote_copy(
            key, given.at[pl.ds(k * tokens, tokens)], gsend.at[0], grecv.at[k],
            device_id=(g, near, t), device_id_type=MESH)

    for i in (1, 2):
        @pl.when(z != i)
        def _():
            table_to(i).start()
            heads_to(i).start()

        @pl.when(z == i)
        def _():
            heads_own(i).start()

    step = 8
    for i in range(groups_of):
        fetch(i).wait()

        def squares(b, carry):
            first = pl.multiple_of(i * per + b * step, step)
            for tap in range(taps):
                total = jnp.zeros((step, block, LANES), jnp.float32)
                for c in range(chunks):
                    x = xbuf[pl.ds(first, step), tap, :, c * LANES:(c + 1) * LANES].astype(jnp.float32)
                    total = total + x * x
                psq[tap, pl.ds(pl.multiple_of(first * block, step * block), step * block), :] = total.reshape(
                    step * block, LANES)
            return carry

        lax.fori_loop(0, per // step, squares, 0)
    sums[0] = jnp.zeros((8, tokens), jnp.float32)
    for tap in range(taps):
        sums[0, tap:tap + 1, :] = jnp.sum(psq[tap].T, axis=0, keepdims=True)

    def sums_to(k):
        return pltpu.make_async_remote_copy(
            sums.at[0], sums.at[k], ssend.at[k - 1], srecv.at[k - 1],
            device_id=(g, z, lax.rem(t + k, 4)), device_id_type=MESH)

    for k in range(1, 4):
        sums_to(k).start()
    for k in range(1, 4):
        sums_to(k).wait()
    inverse = lax.rsqrt((sums[0] + sums[1] + sums[2] + sums[3]) / width + EPSILON)
    for tap in range(taps):
        invb[tap] = jnp.broadcast_to(inverse[tap:tap + 1, :], (LANES, tokens)).T

    def rows_to(c, to, sem):
        here = united.at[c, pl.ds(z * tokens, tokens)]
        return pltpu.make_async_remote_copy(
            here, here, usend.at[sem, c], urecv.at[z, c], device_id=(g, to, t), device_id_type=MESH)

    def rows_from(c, k):
        here = united.at[c, pl.ds(k * tokens, tokens)]
        return pltpu.make_async_remote_copy(
            here, here, usend.at[0, c], urecv.at[k, c], device_id=(g, near, t), device_id_type=MESH)

    def unite(c, carry):
        lanes = pl.ds(pl.multiple_of(c * LANES, LANES), LANES)
        scale = [gain[tap:tap + 1, lanes] for tap in range(taps)]
        for b in range(owned // step):
            total = jnp.zeros((step * block, LANES), jnp.float32)
            for tap in range(taps):
                x = xbuf[b * step:(b + 1) * step, tap, :, lanes].astype(jnp.float32).reshape(step * block, LANES)
                total = total + x * invb[tap, b * step * block:(b + 1) * step * block, :] * scale[tap]
            first = pl.multiple_of(z * tokens + b * step * block, step * block)
            united[c, pl.ds(first, step * block), :] = total.astype(jnp.bfloat16)

        @pl.when(inner)
        def _():
            rows_to(c, partner, 0).start()

        @pl.when(outer)
        def _():
            rows_to(c, far, 0).start()
            rows_to(c, near, 1).start()

        return carry

    lax.fori_loop(0, chunks, unite, 0)

    def slots_to(row, to, sem):
        here = slots.at[pl.ds(row * part, part)]
        return pltpu.make_async_remote_copy(
            here, here, asend.at[sem], arecv.at[sem], device_id=(g, z, to), device_id_type=MESH)

    def back(c, to):
        return pltpu.make_async_remote_copy(
            cbuf.at[c], cbuf.at[c], csend.at[c], crecv.at[c], device_id=(g, to, t), device_id_type=MESH)

    across = lax.rem(t + 2, 4)
    beside = t + 1 - 2 * lax.rem(t, 2)
    opposite = lax.rem(beside + 2, 4)

    @pl.when(inner)
    def _():
        for i in (1, 2):
            @pl.when(z == i)
            def _():
                heads_own(i).wait()
                tabs[i] = tab[...]
                for k in range(4):
                    if k != i:
                        table_from(k).wait_recv()
                        heads_from(k).wait_recv()

        wide = 256

        def by_slot(j, carry):
            first = pl.multiple_of(j * wide, wide)
            place = first + lax.broadcasted_iota(jnp.int32, (wide, tokens), 0)
            total = jnp.zeros((wide, part), jnp.float32)
            for k in range(4):
                chosen = jnp.where(tabs[k, 0:1, :] == place, 1.0, 0.0).astype(jnp.bfloat16)
                total = total + jnp.dot(
                    chosen, given[k * tokens:(k + 1) * tokens, :], preferred_element_type=jnp.float32)
            slots[pl.ds(pl.multiple_of(t * part, part), part), pl.ds(first, wide)] = total.T.astype(jnp.bfloat16)
            return carry

        lax.fori_loop(0, 4 * tokens // wide, by_slot, 0)
        slots_to(t, across, 0).start()
        slots_to(t, beside, 1).start()
        slots_to(across, across, 0).wait_recv()
        slots_to(across, beside, 2).start()
        slots_to(beside, beside, 1).wait_recv()
        slots_to(opposite, beside, 2).wait_recv()

        mine = pl.multiple_of(jnp.where(z == 1, half, 0), half)
        theirs = pl.multiple_of(half - mine, half)

        def product(c, carry):
            for k in range(4):
                @pl.when(z != k)
                def _():
                    rows_from(c, k).wait_recv()
            rows = united[c]
            cbuf[c] = jnp.dot(
                slots[pl.ds(theirs, half), :], rows, preferred_element_type=jnp.float32).astype(jnp.bfloat16)
            back(c, edge).start()
            lanes = pl.ds(pl.multiple_of(c * LANES, LANES), LANES)
            out[:, lanes] = jnp.dot(slots[pl.ds(mine, half), :], rows, preferred_element_type=jnp.float32)
            return carry

        lax.fori_loop(0, chunks, product, 0)

        def sent(c, carry):
            rows_to(c, partner, 0).wait_send()
            back(c, edge).wait_send()
            return carry

        lax.fori_loop(0, chunks, sent, 0)
        slots_to(t, across, 0).wait_send()
        slots_to(t, beside, 1).wait_send()
        slots_to(across, beside, 2).wait_send()

    @pl.when(outer)
    def _():
        def arrive(c, carry):
            back(c, near).wait_recv()
            lanes = pl.ds(pl.multiple_of(c * LANES, LANES), LANES)
            out[:, lanes] = cbuf[c].astype(jnp.float32)
            return carry

        lax.fori_loop(0, chunks, arrive, 0)

        def sent(c, carry):
            rows_to(c, far, 0).wait_send()
            rows_to(c, near, 1).wait_send()
            return carry

        lax.fori_loop(0, chunks, sent, 0)

    for i in (1, 2):
        @pl.when(z != i)
        def _():
            table_to(i).wait_send()
            heads_to(i).wait_send()


def line_body(feature_cache, owner_ids, slot_ids, live_tokens, tap_gain, key_cotangent, value_cotangent):
    owned, block, taps, columns = feature_cache.shape
    tokens = owned * block
    part = key_cotangent.shape[1]
    chunks = columns // LANES
    index = owner_ids[:, 0] * owned + slot_ids
    offsets = jnp.arange(block, dtype=jnp.int32)
    wanted = jnp.where(offsets[None, :] < live_tokens[:, None], index[:, None] * block + offsets, -1)
    tab = jnp.broadcast_to(wanted.reshape(1, tokens), (8, tokens))
    vmem, hbm = pl.BlockSpec(memory_space=pltpu.VMEM), pl.BlockSpec(memory_space=pl.ANY)
    dma = pltpu.SemaphoreType.DMA
    return pl.pallas_call(
        line_kernel,
        out_shape=jax.ShapeDtypeStruct((2 * part, columns), jnp.float32),
        in_specs=[hbm, vmem, vmem, hbm, hbm],
        out_specs=vmem,
        scratch_shapes=[
            pltpu.VMEM((owned, taps, block, columns), jnp.bfloat16),
            pltpu.VMEM((taps, tokens, LANES), jnp.float32),
            pltpu.VMEM((4, 8, tokens), jnp.float32),
            pltpu.VMEM((taps, tokens, LANES), jnp.float32),
            pltpu.VMEM((chunks, 4 * tokens, LANES), jnp.bfloat16),
            pltpu.VMEM((4 * tokens, part), jnp.bfloat16),
            pltpu.VMEM((4, 8, tokens), jnp.int32),
            pltpu.VMEM((4 * part, 4 * tokens), jnp.bfloat16),
            pltpu.VMEM((chunks, 2 * part, LANES), jnp.bfloat16),
            dma((4,)),
            dma((2,)), dma((4,)),
            dma((3,)), dma((4,)),
            dma((3,)), dma((3,)),
            dma((2, chunks)), dma((4, chunks)),
            dma((3,)), dma((3,)),
            dma((chunks,)), dma((chunks,)),
        ],
        compiler_params=pltpu.CompilerParams(
            collective_id=0, has_side_effects=True, vmem_limit_bytes=52 * 2**20),
    )(jnp.transpose(feature_cache, (0, 2, 1, 3)), tab, tap_gain, key_cotangent, value_cotangent)


def solution(mesh):
    in_specs = (
        P(("groups", "dp"), None, None, "tensor"),
        P(("groups", "dp"), None),
        P(("groups", "dp")),
        P(("groups", "dp")),
        P(None, "tensor"),
        P(("groups", "dp"), "tensor"),
        P(("groups", "dp"), "tensor"),
    )
    out_specs = P(("groups", "dp"), "tensor")
    line = mesh.shape["dp"] == 4 and mesh.shape["tensor"] == 4
    body = line_body if line else gather_body
    return jax.shard_map(body, mesh=mesh, in_specs=in_specs, out_specs=out_specs, check_vma=False)
```

```python
import functools

import jax
import jax.numpy as jnp
from jax import lax
from jax.experimental import pallas as pl
from jax.experimental.pallas import tpu as pltpu
from jax.sharding import PartitionSpec as P

EPSILON = 1e-06
MESH = pl.DeviceIdType.MESH
LANES = 128


def united_of(feature_cache, tap_gain, width):
    floats = feature_cache.astype(jnp.float32)
    squares = lax.psum(jnp.sum(floats * floats, axis=-1), "tensor")
    inverse_rms = lax.rsqrt(squares / width + EPSILON)
    return jnp.sum(floats * inverse_rms[..., None] * tap_gain, axis=2).astype(jnp.bfloat16)


def slot_matrix(owner_ids, slot_ids, live_tokens, owned, dtype):
    index = owner_ids[:, 0] * owned + slot_ids
    table = lax.all_gather(jnp.stack([index, live_tokens]), "dp", axis=1, tiled=True)
    slots = lax.axis_size("dp") * owned
    chosen = jnp.arange(slots, dtype=jnp.int32)[:, None] == table[0][None, :]
    return chosen.astype(dtype), table[1]


def gather_body(feature_cache, owner_ids, slot_ids, live_tokens, tap_gain, key_cotangent, value_cotangent):
    owned, block_len, _, columns = feature_cache.shape
    width = columns * lax.axis_size("tensor")
    united = united_of(feature_cache, tap_gain, width).reshape(owned * block_len, columns)
    everywhere = lax.all_gather(united, "dp", axis=0, tiled=True)
    chosen, live = slot_matrix(owner_ids, slot_ids, live_tokens, owned, jnp.bfloat16)
    joined = jnp.concatenate(
        [
            lax.all_gather(key_cotangent, "tensor", axis=1, tiled=True),
            lax.all_gather(value_cotangent, "tensor", axis=1, tiled=True),
        ],
        axis=1,
    )
    mine = lax.all_to_all(joined, "dp", split_axis=1, concat_axis=0, tiled=True)
    rows = mine.shape[1]
    mine = mine.reshape(-1, block_len, rows)
    mask = jnp.arange(block_len, dtype=jnp.int32)[None, :] < live[:, None]
    mine = jnp.where(mask[:, :, None], mine, jnp.zeros_like(mine)).reshape(-1, block_len * rows)
    by_slot = lax.dot_general(
        chosen, mine, (((1,), (0,)), ((), ())), preferred_element_type=jnp.float32
    ).astype(jnp.bfloat16).reshape(-1, rows)
    return lax.dot_general(
        by_slot, everywhere, (((0,), (0,)), ((), ())), preferred_element_type=jnp.float32
    )


def place():
    return tuple(lax.axis_index(n) for n in ("groups", "dp", "tensor"))


def signal_all(barrier, ids):
    for to in ids:
        pl.semaphore_signal(barrier, inc=1, device_id=to, device_id_type=MESH)


def prepare_kernel(
    feats, owner, slot, live, gain_in, key, value,
    united, given, names, ranks, few,
    xbuf, gain, lists, table, tables, columns_of, used, psq, sums, invb, ubuf,
    xsem, lsem, bsend, brecv, gsend, grecv, ssend, srecv, osem,
):
    g, z, t = place()
    owned, taps, block, columns = feats.shape
    tokens = owned * block
    chunks = columns // LANES
    width = columns * 4
    inner = jnp.logical_or(z == 1, z == 2)
    near = jnp.where(z < 2, 1, 2)
    fetches = 4
    per = owned // fetches

    def fetch(i):
        return pltpu.make_async_copy(feats.at[pl.ds(i * per, per)], xbuf.at[pl.ds(i * per, per)], xsem.at[i])

    small = [pltpu.make_async_copy(src, lists.at[i], lsem.at[i]) for i, src in enumerate((owner, slot, live))]
    for copy in small:
        copy.start()
    for i in range(fetches):
        fetch(i).start()
    gains = pltpu.make_async_copy(gain_in, gain, lsem.at[3])
    gains.start()

    barrier = pltpu.get_barrier_semaphore()
    others = [(g, lax.rem(z + k, 4), t) for k in range(1, 4)] + [(1 - g, lax.rem(z + k, 4), t) for k in range(4)]
    signal_all(barrier, others + [(g, z, lax.rem(t + k, 4)) for k in range(1, 4)])
    table[...] = jnp.zeros(table.shape, jnp.int32)
    for i, copy in enumerate(small):
        copy.wait()
        table[i:i + 1, 0:owned] = lists[i]
    pl.semaphore_wait(barrier, 10)

    def table_to(i):
        at = z if i < 3 else 4 + z
        return pltpu.make_async_remote_copy(
            table, tables.at[at], bsend.at[i], brecv.at[at], device_id=others[i], device_id_type=MESH)

    def table_from(at):
        return pltpu.make_async_remote_copy(
            table, tables.at[at], bsend.at[0], brecv.at[at], device_id=others[0], device_id_type=MESH)

    def heads_to(i):
        return pltpu.make_async_remote_copy(
            key if i == 1 else value, given.at[pl.ds(z * tokens, tokens)], gsend.at[i - 1], grecv.at[z],
            device_id=(g, i, t), device_id_type=MESH)

    def heads_own(i):
        return pltpu.make_async_copy(
            key if i == 1 else value, given.at[pl.ds(i * tokens, tokens)], gsend.at[2])

    def heads_from(k):
        return pltpu.make_async_remote_copy(
            key, given.at[pl.ds(k * tokens, tokens)], gsend.at[0], grecv.at[k],
            device_id=(g, near, t), device_id_type=MESH)

    for i in range(7):
        table_to(i).start()
    for i in (1, 2):
        @pl.when(z != i)
        def _():
            heads_to(i).start()

        @pl.when(z == i)
        def _():
            heads_own(i).start()
    tables[z] = table[...]

    step = 8
    for i in range(fetches):
        fetch(i).wait()

        def squares(b, carry):
            first = pl.multiple_of(i * per + b * step, step)
            for tap in range(taps):
                total = jnp.zeros((step, block, LANES), jnp.float32)
                for c in range(chunks):
                    x = xbuf[pl.ds(first, step), tap, :, c * LANES:(c + 1) * LANES].astype(jnp.float32)
                    total = total + x * x
                psq[tap, pl.ds(pl.multiple_of(first * block, step * block), step * block), :] = total.reshape(
                    step * block, LANES)
            return carry

        lax.fori_loop(0, per // step, squares, 0)
    sums[0] = jnp.zeros((8, tokens), jnp.float32)
    for tap in range(taps):
        sums[0, tap:tap + 1, :] = jnp.sum(psq[tap].T, axis=0, keepdims=True)

    def sums_to(k):
        return pltpu.make_async_remote_copy(
            sums.at[0], sums.at[k], ssend.at[k - 1], srecv.at[k - 1],
            device_id=(g, z, lax.rem(t + k, 4)), device_id_type=MESH)

    for k in range(1, 4):
        sums_to(k).start()

    for k in range(1, 4):
        table_from(lax.rem(z + k, 4)).wait_recv()
    for k in range(4):
        table_from(4 + k).wait_recv()
    token = lax.broadcasted_iota(jnp.int32, (LANES, tokens), 1)
    spread = jnp.where(
        lax.div(token, block) == lax.broadcasted_iota(jnp.int32, (LANES, tokens), 0), 1.0, 0.0).astype(jnp.bfloat16)
    offset = lax.rem(lax.broadcasted_iota(jnp.int32, (1, tokens), 1), block)
    for k in range(4):
        entry = jnp.dot(
            tables[k].astype(jnp.float32).astype(jnp.bfloat16), spread, preferred_element_type=jnp.float32
        ).astype(jnp.int32)
        row = (entry[0:1] * owned + entry[1:2]) * block + offset
        names[k] = jnp.broadcast_to(jnp.where(offset < entry[2:3], row, -1), (8, tokens))
    for k in range(8):
        index = (tables[k, 0:1, :] * owned + tables[k, 1:2, :]).astype(jnp.float32)
        columns_of[k, 0] = jnp.broadcast_to(index, (LANES, LANES)).T[0:owned]
        columns_of[k, 1] = jnp.broadcast_to(tables[k, 2:3, :].astype(jnp.float32), (LANES, LANES)).T[0:owned]
    row_chunks = 4 * tokens // LANES

    def mark(c, carry):
        row = c * LANES + lax.broadcasted_iota(jnp.int32, (1, LANES), 1)
        at = lax.div(row, block).astype(jnp.float32)
        for r in range(2):
            most = jnp.zeros((owned, LANES), jnp.float32)
            for k in range(4):
                most = jnp.maximum(most, jnp.where(columns_of[4 * r + k, 0] == at, columns_of[4 * r + k, 1], 0.0))
            most = jnp.max(most, axis=0, keepdims=True)
            used[r, pl.ds(c, 1), :] = jnp.where(lax.rem(row, block).astype(jnp.float32) < most, 1.0, 0.0)
        return carry

    lax.fori_loop(0, row_chunks, mark, 0)
    before = jnp.where(
        lax.broadcasted_iota(jnp.int32, (LANES, LANES), 0) < lax.broadcasted_iota(jnp.int32, (LANES, LANES), 1),
        1.0, 0.0).astype(jnp.bfloat16)
    largest = jnp.zeros((1, LANES), jnp.float32)
    for r in range(2):
        local = jnp.dot(used[r].astype(jnp.bfloat16), before, preferred_element_type=jnp.float32)
        for c in range(row_chunks):
            if c % (row_chunks // 2) == 0:
                run = jnp.zeros((1, LANES), jnp.float32)
            flags = used[r, c:c + 1, :]
            if r == 0:
                rank = jnp.where(flags > 0.0, local[c:c + 1] + run, -1.0).astype(jnp.int32)
                ranks[:, c * LANES:(c + 1) * LANES] = jnp.broadcast_to(rank, (8, LANES))
            run = run + jnp.broadcast_to(jnp.sum(flags, axis=1, keepdims=True), (1, LANES))
            largest = jnp.maximum(largest, run)
    few[...] = jnp.broadcast_to(jnp.where(largest <= float(tokens), 1, 0), few.shape)

    for k in range(1, 4):
        sums_to(k).wait()
    inverse = lax.rsqrt((sums[0] + sums[1] + sums[2] + sums[3]) / width + EPSILON)
    for tap in range(taps):
        invb[tap] = jnp.broadcast_to(inverse[tap:tap + 1, :], (LANES, tokens)).T
    gains.wait()

    def store(c):
        return pltpu.make_async_copy(ubuf.at[c], united.at[c], osem.at[c])

    def unite(c, carry):
        lanes = pl.ds(pl.multiple_of(c * LANES, LANES), LANES)
        scale = [gain[tap:tap + 1, lanes] for tap in range(taps)]
        for b in range(owned // step):
            total = jnp.zeros((step * block, LANES), jnp.float32)
            for tap in range(taps):
                x = xbuf[b * step:(b + 1) * step, tap, :, lanes].astype(jnp.float32).reshape(step * block, LANES)
                total = total + x * invb[tap, b * step * block:(b + 1) * step * block, :] * scale[tap]
            ubuf[c, b * step * block:(b + 1) * step * block, :] = total.astype(jnp.bfloat16)
        store(c).start()
        return carry

    lax.fori_loop(0, chunks, unite, 0)

    def stored(c, carry):
        store(c).wait()
        return carry

    lax.fori_loop(0, chunks, stored, 0)
    for i in (1, 2):
        @pl.when(z == i)
        def _():
            heads_own(i).wait()
            for k in range(4):
                if k != i:
                    heads_from(k).wait_recv()

        @pl.when(z != i)
        def _():
            heads_to(i).wait_send()
    for i in range(7):
        table_to(i).wait_send()


def sum_by_row(names, heads, place_of_first, tokens, part):
    at = place_of_first + lax.broadcasted_iota(jnp.int32, (256, tokens), 0)
    total = jnp.zeros((256, part), jnp.float32)
    for k in range(4):
        chosen = jnp.where(names[k, 0:1, :] == at, 1.0, 0.0).astype(jnp.bfloat16)
        total = total + jnp.dot(chosen, heads[k * tokens:(k + 1) * tokens, :], preferred_element_type=jnp.float32)
    return total


def packed_kernel(
    united, given, names, ranks, out,
    heads, pair, pick, summed, packed, slots, cbuf,
    lsem, nsend, nrecv, psend, precv, asend, arecv, csend, crecv,
):
    g, z, t = place()
    chunks, tokens, _ = united.shape
    part = heads.shape[1]
    half = 2 * part
    inner = jnp.logical_or(z == 1, z == 2)
    side = z - 1
    partner = 3 - z
    near = jnp.where(z < 2, 1, 2)
    edge = jnp.where(z == 1, 0, 3)
    across = lax.rem(t + 2, 4)
    beside = t + 1 - 2 * lax.rem(t, 2)
    opposite = lax.rem(beside + 2, 4)
    barrier = pltpu.get_barrier_semaphore()

    def rows_to(c):
        return pltpu.make_async_remote_copy(
            united.at[c], pair.at[c, pl.ds(lax.rem(z, 2) * tokens, tokens)], nsend.at[c], nrecv.at[c],
            device_id=(g, near, t), device_id_type=MESH)

    def rows_from(c):
        return pltpu.make_async_remote_copy(
            united.at[c], pair.at[c, pl.ds(lax.rem(edge, 2) * tokens, tokens)], nsend.at[c], nrecv.at[c],
            device_id=(g, edge, t), device_id_type=MESH)

    def packed_to(c, which):
        here = packed.at[c, pl.ds(which * tokens, tokens)]
        return pltpu.make_async_remote_copy(
            here, here, psend.at[c], precv.at[c], device_id=(g, partner, t), device_id_type=MESH)

    def slots_to(row, to, sem):
        here = slots.at[pl.ds(row * part, part)]
        return pltpu.make_async_remote_copy(
            here, here, asend.at[sem], arecv.at[sem], device_id=(g, z, to), device_id_type=MESH)

    def back(c, to):
        return pltpu.make_async_remote_copy(
            cbuf.at[c], cbuf.at[c], csend.at[c], crecv.at[c], device_id=(g, to, t), device_id_type=MESH)

    @pl.when(inner)
    def _():
        bring = pltpu.make_async_copy(given, heads, lsem.at[0])
        bring.start()
        own = pltpu.make_async_copy(united, pair.at[:, pl.ds(lax.rem(z, 2) * tokens, tokens)], lsem.at[1])
        own.start()
        signal_all(barrier, [(g, partner, t), (g, edge, t), (g, z, across), (g, z, beside)])

        def choose(h):
            def some(j, carry):
                first = pl.multiple_of(j * 64, 64)
                at = first + lax.broadcasted_iota(jnp.int32, (64, 2 * tokens), 0)
                row = ranks[0:1, h * 2 * tokens:(h + 1) * 2 * tokens]
                pick[h, pl.ds(first, 64), :] = jnp.where(row == at, 1.0, 0.0).astype(jnp.bfloat16)
                return carry

            lax.fori_loop(0, tokens // 64, some, 0)

        bring.wait()
        for h in range(2):
            choose(h)

            def some_rows(j, carry):
                first = pl.multiple_of(j * 256, 256)
                summed[pl.ds(first, 256), :] = sum_by_row(
                    names, heads, h * 2 * tokens + first, tokens, part).astype(jnp.bfloat16)
                return carry

            lax.fori_loop(0, 2 * tokens // 256, some_rows, 0)
            few = jnp.dot(pick[h], summed[...], preferred_element_type=jnp.float32)
            slots[pl.ds(pl.multiple_of(t * part, part), part), h * tokens:(h + 1) * tokens] = few.T.astype(jnp.bfloat16)
        pl.semaphore_wait(barrier, 4)
        slots_to(t, across, 0).start()
        slots_to(t, beside, 1).start()
        own.wait()

        def pack(c):
            rows_from(c).wait_recv()
            few = jnp.dot(pick[side], pair[c], preferred_element_type=jnp.float32)
            packed[c, pl.ds(pl.multiple_of(side * tokens, tokens), tokens), :] = few.astype(jnp.bfloat16)
            packed_to(c, side).start()

        ahead = 4

        def early(c, carry):
            pack(c)
            return carry

        lax.fori_loop(0, ahead, early, 0)
        slots_to(across, across, 0).wait_recv()
        slots_to(across, beside, 2).start()
        pack(ahead)
        slots_to(beside, beside, 1).wait_recv()
        slots_to(opposite, beside, 2).wait_recv()

        mine = pl.multiple_of(jnp.where(z == 1, half, 0), half)
        theirs = pl.multiple_of(half - mine, half)

        def product(c, carry):
            @pl.when(c + ahead + 1 < chunks)
            def _():
                pack(c + ahead + 1)

            packed_to(c, 1 - side).wait_recv()
            rows = packed[c]
            cbuf[c] = jnp.dot(
                slots[pl.ds(theirs, half), :], rows, preferred_element_type=jnp.float32).astype(jnp.bfloat16)
            back(c, edge).start()
            lanes = pl.ds(pl.multiple_of(c * LANES, LANES), LANES)
            out[:, lanes] = jnp.dot(
                slots[pl.ds(mine, half), :], rows, preferred_element_type=jnp.float32).astype(jnp.bfloat16)
            return carry

        lax.fori_loop(0, chunks, product, 0)

        def sent(c, carry):
            packed_to(c, side).wait_send()
            back(c, edge).wait_send()
            return carry

        lax.fori_loop(0, chunks, sent, 0)
        slots_to(t, across, 0).wait_send()
        slots_to(t, beside, 1).wait_send()
        slots_to(across, beside, 2).wait_send()

    @pl.when(jnp.logical_not(inner))
    def _():
        signal_all(barrier, [(g, near, t)])
        pl.semaphore_wait(barrier, 1)

        def give(c, carry):
            rows_to(c).start()
            return carry

        lax.fori_loop(0, chunks, give, 0)

        def arrive(c, carry):
            back(c, near).wait_recv()
            lanes = pl.ds(pl.multiple_of(c * LANES, LANES), LANES)
            out[:, lanes] = cbuf[c]
            return carry

        lax.fori_loop(0, chunks, arrive, 0)

        def sent(c, carry):
            rows_to(c).wait_send()
            return carry

        lax.fori_loop(0, chunks, sent, 0)


def whole_kernel(
    united, given, names, ranks, out,
    heads, everywhere, slots, cbuf,
    lsem, usend, urecv, asend, arecv, csend, crecv,
):
    g, z, t = place()
    chunks, tokens, _ = united.shape
    part = heads.shape[1]
    half = 2 * part
    inner = jnp.logical_or(z == 1, z == 2)
    outer = jnp.logical_not(inner)
    partner = 3 - z
    near = jnp.where(z < 2, 1, 2)
    far = 3 - near
    edge = jnp.where(z == 1, 0, 3)
    beyond = 3 - edge
    across = lax.rem(t + 2, 4)
    beside = t + 1 - 2 * lax.rem(t, 2)
    opposite = lax.rem(beside + 2, 4)
    barrier = pltpu.get_barrier_semaphore()

    def rows_to(c, to, sem):
        return pltpu.make_async_remote_copy(
            united.at[c], everywhere.at[c, pl.ds(z * tokens, tokens)], usend.at[sem, c], urecv.at[z, c],
            device_id=(g, to, t), device_id_type=MESH)

    def rows_from(c, k):
        return pltpu.make_async_remote_copy(
            united.at[c], everywhere.at[c, pl.ds(k * tokens, tokens)], usend.at[0, c], urecv.at[k, c],
            device_id=(g, partner, t), device_id_type=MESH)

    def slots_to(row, to, sem):
        here = slots.at[pl.ds(row * part, part)]
        return pltpu.make_async_remote_copy(
            here, here, asend.at[sem], arecv.at[sem], device_id=(g, z, to), device_id_type=MESH)

    def back(c, to):
        return pltpu.make_async_remote_copy(
            cbuf.at[c], cbuf.at[c], csend.at[c], crecv.at[c], device_id=(g, to, t), device_id_type=MESH)

    @pl.when(inner)
    def _():
        bring = pltpu.make_async_copy(given, heads, lsem.at[0])
        bring.start()
        own = pltpu.make_async_copy(united, everywhere.at[:, pl.ds(z * tokens, tokens)], lsem.at[1])
        own.start()
        signal_all(barrier, [(g, partner, t), (g, edge, t), (g, beyond, t), (g, z, across), (g, z, beside)])
        pl.semaphore_wait(barrier, 5)

        def give(c, carry):
            rows_to(c, partner, 0).start()
            return carry

        lax.fori_loop(0, chunks, give, 0)
        bring.wait()

        def some_rows(j, carry):
            first = pl.multiple_of(j * 256, 256)
            total = sum_by_row(names, heads, first, tokens, part)
            slots[pl.ds(pl.multiple_of(t * part, part), part), pl.ds(first, 256)] = total.T.astype(jnp.bfloat16)
            return carry

        lax.fori_loop(0, 4 * tokens // 256, some_rows, 0)
        slots_to(t, across, 0).start()
        slots_to(t, beside, 1).start()
        own.wait()
        slots_to(across, across, 0).wait_recv()
        slots_to(across, beside, 2).start()
        slots_to(beside, beside, 1).wait_recv()
        slots_to(opposite, beside, 2).wait_recv()

        mine = pl.multiple_of(jnp.where(z == 1, half, 0), half)
        theirs = pl.multiple_of(half - mine, half)

        def product(c, carry):
            for k in range(4):
                @pl.when(z != k)
                def _():
                    rows_from(c, k).wait_recv()
            rows = everywhere[c]
            cbuf[c] = jnp.dot(
                slots[pl.ds(theirs, half), :], rows, preferred_element_type=jnp.float32).astype(jnp.bfloat16)
            back(c, edge).start()
            lanes = pl.ds(pl.multiple_of(c * LANES, LANES), LANES)
            out[:, lanes] = jnp.dot(
                slots[pl.ds(mine, half), :], rows, preferred_element_type=jnp.float32).astype(jnp.bfloat16)
            return carry

        lax.fori_loop(0, chunks, product, 0)

        def sent(c, carry):
            rows_to(c, partner, 0).wait_send()
            back(c, edge).wait_send()
            return carry

        lax.fori_loop(0, chunks, sent, 0)
        slots_to(t, across, 0).wait_send()
        slots_to(t, beside, 1).wait_send()
        slots_to(across, beside, 2).wait_send()

    @pl.when(outer)
    def _():
        signal_all(barrier, [(g, near, t), (g, far, t)])
        pl.semaphore_wait(barrier, 2)

        def give(c, carry):
            rows_to(c, far, 0).start()
            rows_to(c, near, 1).start()
            return carry

        lax.fori_loop(0, chunks, give, 0)

        def arrive(c, carry):
            back(c, near).wait_recv()
            lanes = pl.ds(pl.multiple_of(c * LANES, LANES), LANES)
            out[:, lanes] = cbuf[c]
            return carry

        lax.fori_loop(0, chunks, arrive, 0)

        def sent(c, carry):
            rows_to(c, far, 0).wait_send()
            rows_to(c, near, 1).wait_send()
            return carry

        lax.fori_loop(0, chunks, sent, 0)


def line_body(feature_cache, owner_ids, slot_ids, live_tokens, tap_gain, key_cotangent, value_cotangent):
    owned, block, taps, columns = feature_cache.shape
    tokens = owned * block
    part = key_cotangent.shape[1]
    chunks = columns // LANES
    vmem, hbm = pl.BlockSpec(memory_space=pltpu.VMEM), pl.BlockSpec(memory_space=pltpu.HBM)
    dma = pltpu.SemaphoreType.DMA
    shape = jax.ShapeDtypeStruct

    def params(number, mebibytes):
        return pltpu.CompilerParams(
            collective_id=number, has_side_effects=True, vmem_limit_bytes=mebibytes * 2**20)

    prepared = pl.pallas_call(
        prepare_kernel,
        out_shape=(
            shape((chunks, tokens, LANES), jnp.bfloat16),
            shape((4 * tokens, part), jnp.bfloat16),
            shape((4, 8, tokens), jnp.int32),
            shape((8, 4 * tokens), jnp.int32),
            shape((8, LANES), jnp.int32),
        ),
        in_specs=[hbm] * 7,
        out_specs=(hbm, hbm, vmem, vmem, vmem),
        scratch_shapes=[
            pltpu.VMEM((owned, taps, block, columns), jnp.bfloat16),
            pltpu.VMEM((taps, columns), jnp.float32),
            pltpu.VMEM((3, 1, owned), jnp.int32),
            pltpu.VMEM((8, LANES), jnp.int32),
            pltpu.VMEM((8, 8, LANES), jnp.int32),
            pltpu.VMEM((8, 2, owned, LANES), jnp.float32),
            pltpu.VMEM((2, 4 * tokens // LANES, LANES), jnp.float32),
            pltpu.VMEM((taps, tokens, LANES), jnp.float32),
            pltpu.VMEM((4, 8, tokens), jnp.float32),
            pltpu.VMEM((taps, tokens, LANES), jnp.float32),
            pltpu.VMEM((chunks, tokens, LANES), jnp.bfloat16),
            dma((4,)), dma((4,)),
            dma((7,)), dma((8,)),
            dma((3,)), dma((4,)),
            dma((3,)), dma((3,)),
            dma((chunks,)),
        ],
        compiler_params=params(0, 62),
    )(
        jnp.transpose(feature_cache, (0, 2, 1, 3)), owner_ids.reshape(1, owned), slot_ids.reshape(1, owned),
        live_tokens.reshape(1, owned), tap_gain, key_cotangent, value_cotangent)
    result = shape((2 * part, columns), jnp.bfloat16)

    def packed(*given):
        return pl.pallas_call(
            packed_kernel,
            out_shape=result,
            in_specs=[hbm, hbm, vmem, vmem],
            out_specs=vmem,
            scratch_shapes=[
                pltpu.VMEM((4 * tokens, part), jnp.bfloat16),
                pltpu.VMEM((chunks, 2 * tokens, LANES), jnp.bfloat16),
                pltpu.VMEM((2, tokens, 2 * tokens), jnp.bfloat16),
                pltpu.VMEM((2 * tokens, part), jnp.bfloat16),
                pltpu.VMEM((chunks, 2 * tokens, LANES), jnp.bfloat16),
                pltpu.VMEM((4 * part, 2 * tokens), jnp.bfloat16),
                pltpu.VMEM((chunks, 2 * part, LANES), jnp.bfloat16),
                dma((2,)),
                dma((chunks,)), dma((chunks,)),
                dma((chunks,)), dma((chunks,)),
                dma((3,)), dma((3,)),
                dma((chunks,)), dma((chunks,)),
            ],
            compiler_params=params(1, 40),
        )(*given)

    def whole(*given):
        return pl.pallas_call(
            whole_kernel,
            out_shape=result,
            in_specs=[hbm, hbm, vmem, vmem],
            out_specs=vmem,
            scratch_shapes=[
                pltpu.VMEM((4 * tokens, part), jnp.bfloat16),
                pltpu.VMEM((chunks, 4 * tokens, LANES), jnp.bfloat16),
                pltpu.VMEM((4 * part, 4 * tokens), jnp.bfloat16),
                pltpu.VMEM((chunks, 2 * part, LANES), jnp.bfloat16),
                dma((2,)),
                dma((2, chunks)), dma((4, chunks)),
                dma((3,)), dma((3,)),
                dma((chunks,)), dma((chunks,)),
            ],
            compiler_params=params(2, 40),
        )(*given)

    united, given, names, ranks, few = prepared
    gradient = lax.cond(few[0, 0] > 0, packed, whole, united, given, names, ranks)
    return gradient.astype(jnp.float32)


def solution(mesh):
    in_specs = (
        P(("groups", "dp"), None, None, "tensor"),
        P(("groups", "dp"), None),
        P(("groups", "dp")),
        P(("groups", "dp")),
        P(None, "tensor"),
        P(("groups", "dp"), "tensor"),
        P(("groups", "dp"), "tensor"),
    )
    out_specs = P(("groups", "dp"), "tensor")
    line = tuple(mesh.shape[axis] for axis in ("groups", "dp", "tensor")) == (2, 4, 4)
    body = line_body if line else gather_body
    return jax.shard_map(body, mesh=mesh, in_specs=in_specs, out_specs=out_specs, check_vma=False)
```

```python
import functools

import jax
import jax.numpy as jnp
from jax import lax
from jax.experimental import pallas as pl
from jax.experimental.pallas import tpu as pltpu
from jax.sharding import PartitionSpec as P

EPSILON = 1e-06
MESH = pl.DeviceIdType.MESH
LANES = 128


def united_of(feature_cache, tap_gain, width):
    floats = feature_cache.astype(jnp.float32)
    squares = lax.psum(jnp.sum(floats * floats, axis=-1), "tensor")
    inverse_rms = lax.rsqrt(squares / width + EPSILON)
    return jnp.sum(floats * inverse_rms[..., None] * tap_gain, axis=2).astype(jnp.bfloat16)


def slot_matrix(owner_ids, slot_ids, live_tokens, owned, dtype):
    index = owner_ids[:, 0] * owned + slot_ids
    table = lax.all_gather(jnp.stack([index, live_tokens]), "dp", axis=1, tiled=True)
    slots = lax.axis_size("dp") * owned
    chosen = jnp.arange(slots, dtype=jnp.int32)[:, None] == table[0][None, :]
    return chosen.astype(dtype), table[1]


def gather_body(feature_cache, owner_ids, slot_ids, live_tokens, tap_gain, key_cotangent, value_cotangent):
    owned, block_len, _, columns = feature_cache.shape
    width = columns * lax.axis_size("tensor")
    united = united_of(feature_cache, tap_gain, width).reshape(owned * block_len, columns)
    everywhere = lax.all_gather(united, "dp", axis=0, tiled=True)
    chosen, live = slot_matrix(owner_ids, slot_ids, live_tokens, owned, jnp.bfloat16)
    joined = jnp.concatenate(
        [
            lax.all_gather(key_cotangent, "tensor", axis=1, tiled=True),
            lax.all_gather(value_cotangent, "tensor", axis=1, tiled=True),
        ],
        axis=1,
    )
    mine = lax.all_to_all(joined, "dp", split_axis=1, concat_axis=0, tiled=True)
    rows = mine.shape[1]
    mine = mine.reshape(-1, block_len, rows)
    mask = jnp.arange(block_len, dtype=jnp.int32)[None, :] < live[:, None]
    mine = jnp.where(mask[:, :, None], mine, jnp.zeros_like(mine)).reshape(-1, block_len * rows)
    by_slot = lax.dot_general(
        chosen, mine, (((1,), (0,)), ((), ())), preferred_element_type=jnp.float32
    ).astype(jnp.bfloat16).reshape(-1, rows)
    return lax.dot_general(
        by_slot, everywhere, (((0,), (0,)), ((), ())), preferred_element_type=jnp.float32
    )


def place():
    return tuple(lax.axis_index(n) for n in ("groups", "dp", "tensor"))


def signal_all(barrier, ids):
    for to in ids:
        pl.semaphore_signal(barrier, inc=1, device_id=to, device_id_type=MESH)


def sum_by_row(names, given, first, tokens):
    at = first + lax.broadcasted_iota(jnp.int32, (256, tokens), 0)
    total = jnp.zeros((256, given.shape[1]), jnp.float32)
    for k in range(4):
        chosen = jnp.where(names[k, 0:1, :] == at, 1.0, 0.0).astype(jnp.bfloat16)
        total = total + jnp.dot(chosen, given[k * tokens:(k + 1) * tokens, :], preferred_element_type=jnp.float32)
    return total


def packed_kernel(
    feats, owner, slot, live, gain_in, key, value,
    out, united, given, names, unfit,
    xbuf, gain, lists, table, tables, columns_of, used, ranks, counts, psq, sums, invb,
    pair, chosen, pair_pick, outer_pick, places, packed, slots, cbuf,
    xsem, lsem, bsend, brecv, gsend, grecv, hsem, fsend, frecv, ssend, srecv, osem,
    nsend, nrecv, psend, precv, asend, arecv, csend, crecv,
):
    g, z, t = place()
    owned, taps, block, columns = feats.shape
    tokens = owned * block
    chunks = columns // LANES
    width = columns * 4
    inner = jnp.logical_or(z == 1, z == 2)
    outer = jnp.logical_not(inner)
    room = outer_pick.shape[0]
    limit = pair_pick.shape[0]
    near = jnp.where(z < 2, 1, 2)
    fetches = 4
    per = owned // fetches

    def fetch(i):
        return pltpu.make_async_copy(feats.at[pl.ds(i * per, per)], xbuf.at[pl.ds(i * per, per)], xsem.at[i])

    small = [pltpu.make_async_copy(src, lists.at[i], lsem.at[i]) for i, src in enumerate((owner, slot, live))]
    for copy in small:
        copy.start()
    for i in range(fetches):
        fetch(i).start()
    gains = pltpu.make_async_copy(gain_in, gain, lsem.at[3])
    gains.start()

    barrier = pltpu.get_barrier_semaphore()
    others = [(g, lax.rem(z + k, 4), t) for k in range(1, 4)] + [(1 - g, lax.rem(z + k, 4), t) for k in range(4)]
    signal_all(barrier, others + [(g, z, lax.rem(t + k, 4)) for k in range(1, 4)])
    table[...] = jnp.zeros(table.shape, jnp.int32)
    for i, copy in enumerate(small):
        copy.wait()
        table[i:i + 1, 0:owned] = lists[i]
    pl.semaphore_wait(barrier, 10)

    def table_to(i):
        at = z if i < 3 else 4 + z
        return pltpu.make_async_remote_copy(
            table, tables.at[at], bsend.at[i], brecv.at[at], device_id=others[i], device_id_type=MESH)

    def table_from(at):
        return pltpu.make_async_remote_copy(
            table, tables.at[at], bsend.at[0], brecv.at[at], device_id=others[0], device_id_type=MESH)

    strip = key.shape[1] // 2
    across = lax.rem(t + 2, 4)
    edge = jnp.where(z == 1, 0, 3)
    partner, beyond = 3 - z, 3 - edge

    def heads(i, piece):
        return (key if i == 1 else value).at[:, piece * strip:(piece + 1) * strip]

    def here(k, piece):
        return given.at[pl.ds(k * tokens, tokens), (1 - piece) * strip:(2 - piece) * strip]

    def heads_to(i, piece):
        return pltpu.make_async_remote_copy(
            heads(i, piece), here(z, piece), gsend.at[piece, i - 1], grecv.at[piece, z],
            device_id=(g, i, t), device_id_type=MESH)

    def heads_from(k, piece):
        return pltpu.make_async_remote_copy(
            heads(1, piece), here(k, piece), gsend.at[piece, 0], grecv.at[piece, k],
            device_id=(g, near, t), device_id_type=MESH)

    def heads_own(i, piece):
        return pltpu.make_async_copy(heads(i, piece), here(i, piece), hsem.at[piece])

    def pass_on(src, k):
        return pltpu.make_async_remote_copy(
            src, given.at[pl.ds(k * tokens, tokens), 2 * strip:3 * strip], fsend.at[k], frecv.at[k],
            device_id=(g, z, across), device_id_type=MESH)

    def pass_on_from(k):
        @pl.when(inner)
        def _():
            heads_from(k, 0).wait_recv()
            pass_on(here(k, 0), k).start()

    for i in range(7):
        table_to(i).start()
    for piece in range(2):
        for i in (1, 2):
            @pl.when(z != i)
            def _():
                heads_to(i, piece).start()

            @pl.when(z == i)
            def _():
                heads_own(i, piece).start()
                if piece == 0:
                    pass_on(heads(i, 0), i).start()
    tables[z] = table[...]

    step = 8
    for i in range(fetches):
        fetch(i).wait()

        def squares(b, carry):
            first = pl.multiple_of(i * per + b * step, step)
            for tap in range(taps):
                total = jnp.zeros((step, block, LANES), jnp.float32)
                for c in range(chunks):
                    x = xbuf[pl.ds(first, step), tap, :, c * LANES:(c + 1) * LANES].astype(jnp.float32)
                    total = total + x * x
                psq[tap, pl.ds(pl.multiple_of(first * block, step * block), step * block), :] = total.reshape(
                    step * block, LANES)
            return carry

        lax.fori_loop(0, per // step, squares, 0)
    sums[0] = jnp.zeros((8, tokens), jnp.float32)
    for tap in range(taps):
        sums[0, tap:tap + 1, :] = jnp.sum(psq[tap].T, axis=0, keepdims=True)

    def sums_to(k):
        return pltpu.make_async_remote_copy(
            sums.at[0], sums.at[k], ssend.at[k - 1], srecv.at[k - 1],
            device_id=(g, z, lax.rem(t + k, 4)), device_id_type=MESH)

    for k in range(1, 4):
        sums_to(k).start()

    for k in range(1, 4):
        table_from(lax.rem(z + k, 4)).wait_recv()
    for k in range(4):
        table_from(4 + k).wait_recv()
    for k in range(8):
        index = (tables[k, 0:1, :] * owned + tables[k, 1:2, :]).astype(jnp.float32)
        columns_of[k, 0] = jnp.broadcast_to(index, (LANES, LANES)).T[0:owned]
        columns_of[k, 1] = jnp.broadcast_to(tables[k, 2:3, :].astype(jnp.float32), (LANES, LANES)).T[0:owned]

    def most_of(r, at):
        most = jnp.zeros((owned, LANES), jnp.float32)
        for k in range(4):
            most = jnp.maximum(most, jnp.where(columns_of[4 * r + k, 0] == at, columns_of[4 * r + k, 1], 0.0))
        return jnp.max(most, axis=0, keepdims=True)

    blocks = 4 * owned
    most = jnp.concatenate([
        most_of(0, (n * LANES + lax.broadcasted_iota(jnp.int32, (1, LANES), 1)).astype(jnp.float32))
        for n in range(blocks // LANES)], axis=1)
    most = jnp.broadcast_to(most, (8, blocks)).astype(jnp.bfloat16)
    token = lax.broadcasted_iota(jnp.int32, (LANES, tokens), 1)
    spread = jnp.where(
        lax.div(token, block) == lax.broadcasted_iota(jnp.int32, (LANES, tokens), 0), 1.0, 0.0).astype(jnp.bfloat16)
    offset = lax.rem(lax.broadcasted_iota(jnp.int32, (1, tokens), 1), block)
    for k in range(4):
        index = tables[k, 0:1, :] * owned + tables[k, 1:2, :]
        other = lax.broadcasted_iota(jnp.int32, (blocks, LANES), 0)
        ahead_of = jnp.where(
            jnp.logical_and(other < index, other >= jnp.where(index < blocks // 2, 0, blocks // 2)), 1.0, 0.0)
        rows_ahead = jnp.dot(most, ahead_of.astype(jnp.bfloat16), preferred_element_type=jnp.float32)[0:1].astype(jnp.int32)
        high = lax.div(rows_ahead, 64)
        entry = jnp.concatenate(
            [tables[k, 0:3, :], high, rows_ahead - 64 * high, jnp.zeros((3, LANES), jnp.int32)], axis=0)
        entry = jnp.dot(
            entry.astype(jnp.float32).astype(jnp.bfloat16), spread, preferred_element_type=jnp.float32
        ).astype(jnp.int32)
        alive = offset < entry[2:3]
        row = (entry[0:1] * owned + entry[1:2]) * block + offset
        names[k] = jnp.broadcast_to(jnp.where(alive, row, -1), (8, tokens))
        within = entry[3:4] * 64 + entry[4:5] + offset
        alive = jnp.logical_and(alive, within < limit)
        places[k] = jnp.broadcast_to(
            jnp.where(alive, within + jnp.where(entry[0:1] < 2, 0, limit), -1), (8, tokens))
    row_chunks = 4 * tokens // LANES

    def mark(c, carry):
        row = c * LANES + lax.broadcasted_iota(jnp.int32, (1, LANES), 1)
        at = lax.div(row, block).astype(jnp.float32)
        for r in range(2):
            most = most_of(r, at)
            used[r, pl.ds(c, 1), :] = jnp.where(lax.rem(row, block).astype(jnp.float32) < most, 1.0, 0.0)
        return carry

    lax.fori_loop(0, row_chunks, mark, 0)
    before = jnp.where(
        lax.broadcasted_iota(jnp.int32, (LANES, LANES), 0) < lax.broadcasted_iota(jnp.int32, (LANES, LANES), 1),
        1.0, 0.0).astype(jnp.bfloat16)
    excess = jnp.full((1, LANES), -1.0, jnp.float32)
    zero = jnp.zeros((1, LANES), jnp.float32)
    for r in range(2):
        local = jnp.dot(used[r].astype(jnp.bfloat16), before, preferred_element_type=jnp.float32)
        for c in range(row_chunks):
            if c % (row_chunks // 2) == 0:
                base = zero
            if c % (row_chunks // 4) == 0:
                run = zero
            flags = used[r, c:c + 1, :]
            if r == 0:
                rank = jnp.where(flags > 0.0, local[c:c + 1] + run, -1.0)
                at = slice(c * LANES, (c + 1) * LANES)
                ranks[0, :, at] = jnp.broadcast_to(jnp.where(flags > 0.0, rank + base, -1.0).astype(jnp.int32), (8, LANES))
                ranks[1, :, at] = jnp.broadcast_to(rank.astype(jnp.int32), (8, LANES))
            run = run + jnp.broadcast_to(jnp.sum(flags, axis=1, keepdims=True), (1, LANES))
            if (c + 1) % (row_chunks // 4) == 0:
                which = c // (row_chunks // 4)
                if r == 0:
                    counts[which] = jnp.broadcast_to(run.astype(jnp.int32), (8, LANES))
                if which in (0, 3):
                    excess = jnp.maximum(excess, run - float(room))
                base = base + run
                excess = jnp.maximum(excess, base - float(limit))
    unfit[0, 0] = jnp.max(excess).astype(jnp.int32)

    def one_hot(to, count, row):
        def some(n, carry):
            first = pl.multiple_of(n * 64, 64)
            at = first + lax.broadcasted_iota(jnp.int32, (64, row.shape[1]), 0)
            to[pl.ds(first, 64), :] = jnp.where(row == at, 1.0, 0.0).astype(jnp.bfloat16)
            return carry

        lax.fori_loop(0, count // 64, some, 0)

    own_rows = pl.ds(pl.multiple_of(z * tokens, tokens), tokens)

    @pl.when(outer)
    def _():
        one_hot(outer_pick, room, ranks[1, 0:1, own_rows])

    pass_on_from(edge)
    for k in range(1, 4):
        sums_to(k).wait()
    inverse = lax.rsqrt((sums[0] + sums[1] + sums[2] + sums[3]) / width + EPSILON)
    for tap in range(taps):
        invb[tap] = jnp.broadcast_to(inverse[tap:tap + 1, :], (LANES, tokens)).T
    gains.wait()

    def store(c):
        return pltpu.make_async_copy(pair.at[c, 0:tokens], united.at[c], osem.at[c])

    def rows_to(c):
        return pltpu.make_async_remote_copy(
            packed.at[c, 0:room], pair.at[c, tokens:tokens + room], nsend.at[c], nrecv.at[c],
            device_id=(g, near, t), device_id_type=MESH)

    def unite(c, carry):
        lanes = pl.ds(pl.multiple_of(c * LANES, LANES), LANES)
        scale = [gain[tap:tap + 1, lanes] for tap in range(taps)]
        for b in range(owned // step):
            total = jnp.zeros((step * block, LANES), jnp.float32)
            for tap in range(taps):
                x = xbuf[b * step:(b + 1) * step, tap, :, lanes].astype(jnp.float32).reshape(step * block, LANES)
                total = total + x * invb[tap, b * step * block:(b + 1) * step * block, :] * scale[tap]
            pair[c, b * step * block:(b + 1) * step * block, :] = total.astype(jnp.bfloat16)
        store(c).start()

        @pl.when(outer)
        def _():
            packed[c, 0:room, :] = jnp.dot(
                outer_pick[...], pair[c, 0:tokens, :], preferred_element_type=jnp.float32).astype(jnp.bfloat16)
            rows_to(c).start()

        return carry

    lax.fori_loop(0, chunks // 2, unite, 0)
    pass_on_from(partner)
    lax.fori_loop(chunks // 2, chunks, unite, 0)
    pass_on_from(beyond)

    part = 2 * strip
    side = z - 1
    beside = t + 1 - 2 * lax.rem(t, 2)
    opposite = lax.rem(beside + 2, 4)

    def packed_to(c, which):
        here = packed.at[c, pl.ds(which * limit, limit)]
        return pltpu.make_async_remote_copy(
            here, here, psend.at[c], precv.at[c], device_id=(g, partner, t), device_id_type=MESH)

    def slots_to(row, piece, to, sem):
        here = slots.at[piece, pl.ds(row * strip, strip)]
        return pltpu.make_async_remote_copy(
            here, here, asend.at[sem + piece], arecv.at[sem + piece], device_id=(g, z, to), device_id_type=MESH)

    def back(c, piece, to):
        here = cbuf.at[c, piece]
        return pltpu.make_async_remote_copy(
            here, here, csend.at[piece, c], crecv.at[piece, c], device_id=(g, to, t), device_id_type=MESH)

    def back_whole(c, to):
        here = cbuf.at[c]
        return pltpu.make_async_remote_copy(
            here, here, csend.at[0, c], crecv.at[0, c], device_id=(g, to, t), device_id_type=MESH)

    @pl.when(inner)
    def _():
        outer_rank = lax.broadcasted_iota(jnp.int32, (1, room), 1)
        outer_count = jnp.concatenate([counts[edge, 0:1, :]] * (room // LANES), axis=1)
        outer_base = jnp.concatenate([jnp.where(z == 1, 0, counts[2, 0:1, :])] * (room // LANES), axis=1)
        one_hot(pair_pick, limit, jnp.concatenate([
            ranks[0, 0:1, own_rows], jnp.where(outer_rank < outer_count, outer_rank + outer_base, -1)], axis=1))

        def choose(n, carry):
            first = pl.multiple_of(n * 64, 64)
            at = first + lax.broadcasted_iota(jnp.int32, (64, tokens), 0)
            for k in range(4):
                chosen[pl.ds(first, 64), k * tokens:(k + 1) * tokens] = jnp.where(
                    places[k, 0:1, :] == at, 1.0, 0.0).astype(jnp.bfloat16)
            return carry

        lax.fori_loop(0, 2 * limit // 64, choose, 0)

        def strip_of(piece, row):
            return piece, pl.ds(pl.multiple_of(row * strip, strip), strip)

        def heads_arrive(piece):
            for i in (1, 2):
                @pl.when(z == i)
                def _():
                    heads_own(i, piece).wait()
                    for k in range(4):
                        if piece == 0:
                            pass_on(here(k, 0), k).wait()
                        elif k != i:
                            heads_from(k, 1).wait_recv()

        def sum_first(n, carry):
            rows = pl.ds(pl.multiple_of(n * 384, 384), 384)
            some = jnp.dot(chosen[rows, :], given[:, strip:3 * strip], preferred_element_type=jnp.float32)
            some = some.T.astype(jnp.bfloat16)
            slots[(*strip_of(0, t), rows)] = some[0:strip]
            slots[(*strip_of(0, across), rows)] = some[strip:2 * strip]
            return carry

        def sum_second(n, carry):
            rows = pl.ds(pl.multiple_of(n * 384, 384), 384)
            some = jnp.dot(chosen[rows, :], given[:, 0:strip], preferred_element_type=jnp.float32)
            slots[(*strip_of(1, t), rows)] = some.T.astype(jnp.bfloat16)
            return carry

        def pack(c):
            rows_to(c).wait_recv()
            few = jnp.dot(pair_pick[...], pair[c], preferred_element_type=jnp.float32)
            packed[c, pl.ds(pl.multiple_of(side * limit, limit), limit), :] = few.astype(jnp.bfloat16)
            packed_to(c, side).start()

        mine = pl.multiple_of(jnp.where(z == 1, part, 0), part)
        theirs = pl.multiple_of(part - mine, part)

        def send_back(c, piece, go=True):
            cbuf[c, piece] = jnp.dot(
                slots[piece, pl.ds(theirs, part), :], packed[c], preferred_element_type=jnp.float32
            ).astype(jnp.bfloat16)
            if go:
                back(c, piece, edge).start()

        def keep(c):
            lanes = pl.ds(pl.multiple_of(c * LANES, LANES), LANES)
            for piece in range(2):
                rows = jnp.dot(
                    slots[piece, pl.ds(mine, part), :], packed[c], preferred_element_type=jnp.float32
                ).astype(jnp.bfloat16)
                for which in range(2):
                    first = which * part + piece * strip
                    out[first:first + strip, lanes] = rows[which * strip:(which + 1) * strip]

        def gathered(piece):
            if piece == 1:
                slots_to(across, piece, across, 0).wait_recv()
                slots_to(across, piece, beside, 4).start()
            slots_to(beside, piece, beside, 2).wait_recv()
            slots_to(opposite, piece, beside, 4).wait_recv()

        heads_arrive(0)
        lax.fori_loop(0, 2 * limit // 384, sum_first, 0)
        slots_to(t, 0, beside, 2).start()
        slots_to(across, 0, beside, 4).start()
        pack(0)
        heads_arrive(1)
        lax.fori_loop(0, 2 * limit // 384, sum_second, 0)
        slots_to(t, 1, across, 0).start()
        slots_to(t, 1, beside, 2).start()

        early, ahead = 1, 3
        for c in range(1, ahead):
            pack(c)
        gathered(0)
        for c in range(early):
            packed_to(c, 1 - side).wait_recv()
            send_back(c, 0)
            pack(c + ahead)
        gathered(1)
        for c in range(early):
            send_back(c, 1)

        def product(c, carry):
            packed_to(c, 1 - side).wait_recv()
            for piece in range(2):
                send_back(c, piece, False)
            back_whole(c, edge).start()

            @pl.when(c + ahead < chunks)
            def _():
                pack(c + ahead)

            keep(c - early)
            return carry

        lax.fori_loop(early, chunks, product, 0)

        def last(c, carry):
            keep(c)
            return carry

        lax.fori_loop(chunks - early, chunks, last, 0)

        def sent(c, carry):
            packed_to(c, side).wait_send()
            return carry

        lax.fori_loop(0, chunks, sent, 0)
        for c in range(early):
            for piece in range(2):
                back(c, piece, edge).wait_send()

        def sent_whole(c, carry):
            back_whole(c, edge).wait_send()
            return carry

        lax.fori_loop(early, chunks, sent_whole, 0)
        slots_to(t, 1, across, 0).wait_send()
        for piece in range(2):
            slots_to(t, piece, beside, 2).wait_send()
            slots_to(across, piece, beside, 4).wait_send()

    @pl.when(outer)
    def _():
        def place_rows(c, piece):
            lanes = pl.ds(pl.multiple_of(c * LANES, LANES), LANES)
            for which in range(2):
                first = which * part + piece * strip
                out[first:first + strip, lanes] = cbuf[c, piece, which * strip:(which + 1) * strip]

        for c in range(1):
            for piece in range(2):
                back(c, piece, near).wait_recv()
                place_rows(c, piece)

        def arrive(c, carry):
            back_whole(c, near).wait_recv()
            for piece in range(2):
                place_rows(c, piece)
            return carry

        lax.fori_loop(1, chunks, arrive, 0)

        def sent(c, carry):
            rows_to(c).wait_send()
            return carry

        lax.fori_loop(0, chunks, sent, 0)

    def stored(c, carry):
        store(c).wait()
        return carry

    lax.fori_loop(0, chunks, stored, 0)
    for i in (1, 2):
        @pl.when(z != i)
        def _():
            for piece in range(2):
                heads_to(i, piece).wait_send()
    for i in range(7):
        table_to(i).wait_send()


def whole_kernel(
    united, given, names, out,
    everywhere, slots, cbuf,
    lsem, usend, urecv, asend, arecv, csend, crecv,
):
    g, z, t = place()
    chunks, tokens, _ = united.shape
    strip = given.shape[1] // 3
    part = 2 * strip
    half = 2 * part
    inner = jnp.logical_or(z == 1, z == 2)
    outer = jnp.logical_not(inner)
    partner = 3 - z
    near = jnp.where(z < 2, 1, 2)
    far = 3 - near
    edge = jnp.where(z == 1, 0, 3)
    beyond = 3 - edge
    across = lax.rem(t + 2, 4)
    beside = t + 1 - 2 * lax.rem(t, 2)
    opposite = lax.rem(beside + 2, 4)
    barrier = pltpu.get_barrier_semaphore()

    def rows_to(c, to, sem):
        return pltpu.make_async_remote_copy(
            united.at[c], everywhere.at[c, pl.ds(z * tokens, tokens)], usend.at[sem, c], urecv.at[z, c],
            device_id=(g, to, t), device_id_type=MESH)

    def rows_from(c, k):
        return pltpu.make_async_remote_copy(
            united.at[c], everywhere.at[c, pl.ds(k * tokens, tokens)], usend.at[0, c], urecv.at[k, c],
            device_id=(g, partner, t), device_id_type=MESH)

    def slots_to(row, to, sem):
        here = slots.at[pl.ds(row * part, part)]
        return pltpu.make_async_remote_copy(
            here, here, asend.at[sem], arecv.at[sem], device_id=(g, z, to), device_id_type=MESH)

    def back(c, to):
        return pltpu.make_async_remote_copy(
            cbuf.at[c], cbuf.at[c], csend.at[c], crecv.at[c], device_id=(g, to, t), device_id_type=MESH)

    @pl.when(inner)
    def _():
        own = pltpu.make_async_copy(united, everywhere.at[:, pl.ds(z * tokens, tokens)], lsem.at[0])
        own.start()
        signal_all(barrier, [(g, partner, t), (g, edge, t), (g, beyond, t), (g, z, across), (g, z, beside)])
        pl.semaphore_wait(barrier, 5)

        def give(c, carry):
            rows_to(c, partner, 0).start()
            return carry

        lax.fori_loop(0, chunks, give, 0)

        def some_rows(j, carry):
            first = pl.multiple_of(j * 256, 256)
            total = sum_by_row(names, given, first, tokens).T.astype(jnp.bfloat16)
            for piece in range(2):
                slots[pl.ds(pl.multiple_of(t * part + piece * strip, strip), strip), pl.ds(first, 256)] = total[
                    (1 - piece) * strip:(2 - piece) * strip]
            return carry

        lax.fori_loop(0, 4 * tokens // 256, some_rows, 0)
        slots_to(t, across, 0).start()
        slots_to(t, beside, 1).start()
        own.wait()
        slots_to(across, across, 0).wait_recv()
        slots_to(across, beside, 2).start()
        slots_to(beside, beside, 1).wait_recv()
        slots_to(opposite, beside, 2).wait_recv()

        mine = pl.multiple_of(jnp.where(z == 1, half, 0), half)
        theirs = pl.multiple_of(half - mine, half)

        def product(c, carry):
            for k in range(4):
                @pl.when(z != k)
                def _():
                    rows_from(c, k).wait_recv()
            rows = everywhere[c]
            cbuf[c] = jnp.dot(
                slots[pl.ds(theirs, half), :], rows, preferred_element_type=jnp.float32).astype(jnp.bfloat16)
            back(c, edge).start()
            lanes = pl.ds(pl.multiple_of(c * LANES, LANES), LANES)
            out[:, lanes] = jnp.dot(
                slots[pl.ds(mine, half), :], rows, preferred_element_type=jnp.float32).astype(jnp.bfloat16)
            return carry

        lax.fori_loop(0, chunks, product, 0)

        def sent(c, carry):
            rows_to(c, partner, 0).wait_send()
            back(c, edge).wait_send()
            return carry

        lax.fori_loop(0, chunks, sent, 0)
        slots_to(t, across, 0).wait_send()
        slots_to(t, beside, 1).wait_send()
        slots_to(across, beside, 2).wait_send()

    @pl.when(outer)
    def _():
        signal_all(barrier, [(g, near, t), (g, far, t)])
        pl.semaphore_wait(barrier, 2)

        def give(c, carry):
            rows_to(c, far, 0).start()
            rows_to(c, near, 1).start()
            return carry

        lax.fori_loop(0, chunks, give, 0)

        def arrive(c, carry):
            back(c, near).wait_recv()
            lanes = pl.ds(pl.multiple_of(c * LANES, LANES), LANES)
            out[:, lanes] = cbuf[c]
            return carry

        lax.fori_loop(0, chunks, arrive, 0)

        def sent(c, carry):
            rows_to(c, far, 0).wait_send()
            rows_to(c, near, 1).wait_send()
            return carry

        lax.fori_loop(0, chunks, sent, 0)


def line_body(feature_cache, owner_ids, slot_ids, live_tokens, tap_gain, key_cotangent, value_cotangent):
    owned, block, taps, columns = feature_cache.shape
    tokens = owned * block
    part = key_cotangent.shape[1]
    chunks = columns // LANES
    vmem, hbm = pl.BlockSpec(memory_space=pltpu.VMEM), pl.BlockSpec(memory_space=pltpu.HBM)
    dma = pltpu.SemaphoreType.DMA
    shape = jax.ShapeDtypeStruct

    def params(number, mebibytes):
        return pltpu.CompilerParams(
            collective_id=number, has_side_effects=True, vmem_limit_bytes=mebibytes * 2**20)

    room, limit = 3 * tokens // 4, 9 * tokens // 8
    shapes = (
        shape((2 * part, columns), jnp.bfloat16),
        shape((chunks, tokens, LANES), jnp.bfloat16),
        shape((4 * tokens, part + part // 2), jnp.bfloat16),
        shape((4, 8, tokens), jnp.int32),
        shape((1, 1), jnp.int32),
    )
    gradient, united, given, names, unfit = pl.pallas_call(
        packed_kernel,
        out_shape=shapes,
        in_specs=[hbm] * 7,
        out_specs=(vmem, hbm, vmem, vmem, pl.BlockSpec(memory_space=pltpu.SMEM)),
        scratch_shapes=[
            pltpu.VMEM((owned, taps, block, columns), jnp.bfloat16),
            pltpu.VMEM((taps, columns), jnp.float32),
            pltpu.VMEM((3, 1, owned), jnp.int32),
            pltpu.VMEM((8, LANES), jnp.int32),
            pltpu.VMEM((8, 8, LANES), jnp.int32),
            pltpu.VMEM((8, 2, owned, LANES), jnp.float32),
            pltpu.VMEM((2, 4 * tokens // LANES, LANES), jnp.float32),
            pltpu.VMEM((2, 8, 4 * tokens), jnp.int32),
            pltpu.VMEM((4, 8, LANES), jnp.int32),
            pltpu.VMEM((taps, tokens, LANES), jnp.float32),
            pltpu.VMEM((4, 8, tokens), jnp.float32),
            pltpu.VMEM((taps, tokens, LANES), jnp.float32),
            pltpu.VMEM((chunks, tokens + room, LANES), jnp.bfloat16),
            pltpu.VMEM((2 * limit, 4 * tokens), jnp.bfloat16),
            pltpu.VMEM((limit, tokens + room), jnp.bfloat16),
            pltpu.VMEM((room, tokens), jnp.bfloat16),
            pltpu.VMEM((4, 8, tokens), jnp.int32),
            pltpu.VMEM((chunks, 2 * limit, LANES), jnp.bfloat16),
            pltpu.VMEM((2, 2 * part, 2 * limit), jnp.bfloat16),
            pltpu.VMEM((chunks, 2, part, LANES), jnp.bfloat16),
            dma((4,)), dma((4,)),
            dma((7,)), dma((8,)),
            dma((2, 2)), dma((2, 4)), dma((2,)),
            dma((4,)), dma((4,)),
            dma((3,)), dma((3,)),
            dma((chunks,)),
            dma((chunks,)), dma((chunks,)),
            dma((chunks,)), dma((chunks,)),
            dma((6,)), dma((6,)),
            dma((2, chunks)), dma((2, chunks)),
        ],
        compiler_params=params(0, 58),
    )(
        jnp.transpose(feature_cache, (0, 2, 1, 3)), owner_ids.reshape(1, owned), slot_ids.reshape(1, owned),
        live_tokens.reshape(1, owned), tap_gain, key_cotangent, value_cotangent)

    def whole(_, *given):
        return pl.pallas_call(
            whole_kernel,
            out_shape=shapes[0],
            in_specs=[hbm, vmem, vmem],
            out_specs=vmem,
            scratch_shapes=[
                pltpu.VMEM((chunks, 4 * tokens, LANES), jnp.bfloat16),
                pltpu.VMEM((4 * part, 4 * tokens), jnp.bfloat16),
                pltpu.VMEM((chunks, 2 * part, LANES), jnp.bfloat16),
                dma((1,)),
                dma((2, chunks)), dma((4, chunks)),
                dma((3,)), dma((3,)),
                dma((chunks,)), dma((chunks,)),
            ],
            compiler_params=params(1, 40),
        )(*given).astype(jnp.float32)

    def fits(gradient, *_):
        return gradient.astype(jnp.float32)

    return lax.cond(unfit[0, 0] <= 0, fits, whole, gradient, united, given, names)


def solution(mesh):
    in_specs = (
        P(("groups", "dp"), None, None, "tensor"),
        P(("groups", "dp"), None),
        P(("groups", "dp")),
        P(("groups", "dp")),
        P(None, "tensor"),
        P(("groups", "dp"), "tensor"),
        P(("groups", "dp"), "tensor"),
    )
    out_specs = P(("groups", "dp"), "tensor")
    line = tuple(mesh.shape[axis] for axis in ("groups", "dp", "tensor")) == (2, 4, 4)
    body = line_body if line else gather_body
    return jax.shard_map(body, mesh=mesh, in_specs=in_specs, out_specs=out_specs, check_vma=False)
```

```python
import functools

import jax
import jax.numpy as jnp
from jax import lax
from jax.experimental import pallas as pl
from jax.experimental.pallas import tpu as pltpu
from jax.sharding import PartitionSpec as P

EPSILON = 1e-06
MESH = pl.DeviceIdType.MESH
LANES = 128


def united_of(feature_cache, tap_gain, width):
    floats = feature_cache.astype(jnp.float32)
    squares = lax.psum(jnp.sum(floats * floats, axis=-1), "tensor")
    inverse_rms = lax.rsqrt(squares / width + EPSILON)
    return jnp.sum(floats * inverse_rms[..., None] * tap_gain, axis=2).astype(jnp.bfloat16)


def slot_matrix(owner_ids, slot_ids, live_tokens, owned, dtype):
    index = owner_ids[:, 0] * owned + slot_ids
    table = lax.all_gather(jnp.stack([index, live_tokens]), "dp", axis=1, tiled=True)
    slots = lax.axis_size("dp") * owned
    chosen = jnp.arange(slots, dtype=jnp.int32)[:, None] == table[0][None, :]
    return chosen.astype(dtype), table[1]


def gather_body(feature_cache, owner_ids, slot_ids, live_tokens, tap_gain, key_cotangent, value_cotangent):
    owned, block_len, _, columns = feature_cache.shape
    width = columns * lax.axis_size("tensor")
    united = united_of(feature_cache, tap_gain, width).reshape(owned * block_len, columns)
    everywhere = lax.all_gather(united, "dp", axis=0, tiled=True)
    chosen, live = slot_matrix(owner_ids, slot_ids, live_tokens, owned, jnp.bfloat16)
    joined = jnp.concatenate(
        [
            lax.all_gather(key_cotangent, "tensor", axis=1, tiled=True),
            lax.all_gather(value_cotangent, "tensor", axis=1, tiled=True),
        ],
        axis=1,
    )
    mine = lax.all_to_all(joined, "dp", split_axis=1, concat_axis=0, tiled=True)
    rows = mine.shape[1]
    mine = mine.reshape(-1, block_len, rows)
    mask = jnp.arange(block_len, dtype=jnp.int32)[None, :] < live[:, None]
    mine = jnp.where(mask[:, :, None], mine, jnp.zeros_like(mine)).reshape(-1, block_len * rows)
    by_slot = lax.dot_general(
        chosen, mine, (((1,), (0,)), ((), ())), preferred_element_type=jnp.float32
    ).astype(jnp.bfloat16).reshape(-1, rows)
    return lax.dot_general(
        by_slot, everywhere, (((0,), (0,)), ((), ())), preferred_element_type=jnp.float32
    )


def place():
    return tuple(lax.axis_index(n) for n in ("groups", "dp", "tensor"))


def signal_all(barrier, ids):
    for to in ids:
        pl.semaphore_signal(barrier, inc=1, device_id=to, device_id_type=MESH)


def sum_by_row(names, given, first, tokens):
    at = first + lax.broadcasted_iota(jnp.int32, (256, tokens), 0)
    total = jnp.zeros((256, given.shape[1]), jnp.float32)
    for k in range(4):
        chosen = jnp.where(names[k, 0:1, :] == at, 1.0, 0.0).astype(jnp.bfloat16)
        total = total + jnp.dot(chosen, given[k * tokens:(k + 1) * tokens, :], preferred_element_type=jnp.float32)
    return total


def packed_kernel(
    feats, owner, slot, live, gain_in, key, value,
    out, united, given_out, names, unfit,
    given, xbuf, gain, lists, table, tables, columns_of, used, ranks, counts, psq, sums, invb,
    pair, chosen, pair_pick, outer_pick, places, packed, slots, cbuf,
    xsem, lsem, bsend, brecv, gsend, grecv, hsem, fsend, frecv, ssend, srecv, osem, dsem,
    nsend, nrecv, psend, precv, asend, arecv, csend, crecv,
):
    g, z, t = place()
    owned, taps, block, columns = feats.shape
    tokens = owned * block
    chunks = columns // LANES
    width = columns * 4
    inner = jnp.logical_or(z == 1, z == 2)
    outer = jnp.logical_not(inner)
    room = outer_pick.shape[0]
    limit = pair_pick.shape[0]
    near = jnp.where(z < 2, 1, 2)
    fetches = 4
    per = owned // fetches

    def fetch(i):
        return pltpu.make_async_copy(feats.at[pl.ds(i * per, per)], xbuf.at[pl.ds(i * per, per)], xsem.at[i])

    small = [pltpu.make_async_copy(src, lists.at[i], lsem.at[i]) for i, src in enumerate((owner, slot, live))]
    for copy in small:
        copy.start()
    for i in range(fetches):
        fetch(i).start()
    gains = pltpu.make_async_copy(gain_in, gain, lsem.at[3])
    gains.start()

    barrier = pltpu.get_barrier_semaphore()
    others = [(g, lax.rem(z + k, 4), t) for k in range(1, 4)] + [(1 - g, lax.rem(z + k, 4), t) for k in range(4)]
    signal_all(barrier, others + [(g, z, lax.rem(t + k, 4)) for k in range(1, 4)])
    table[...] = jnp.zeros(table.shape, jnp.int32)
    for i, copy in enumerate(small):
        copy.wait()
        table[i:i + 1, 0:owned] = lists[i]
    pl.semaphore_wait(barrier, 10)

    def table_to(i):
        at = z if i < 3 else 4 + z
        return pltpu.make_async_remote_copy(
            table, tables.at[at], bsend.at[i], brecv.at[at], device_id=others[i], device_id_type=MESH)

    def table_from(at):
        return pltpu.make_async_remote_copy(
            table, tables.at[at], bsend.at[0], brecv.at[at], device_id=others[0], device_id_type=MESH)

    strip = key.shape[1] // 2
    across = lax.rem(t + 2, 4)
    edge = jnp.where(z == 1, 0, 3)
    partner, beyond = 3 - z, 3 - edge

    def heads(i, piece):
        return (key if i == 1 else value).at[:, piece * strip:(piece + 1) * strip]

    def here(k, piece):
        return given.at[pl.ds(k * tokens, tokens), (1 - piece) * strip:(2 - piece) * strip]

    def heads_to(i, piece):
        return pltpu.make_async_remote_copy(
            heads(i, piece), here(z, piece), gsend.at[piece, i - 1], grecv.at[piece, z],
            device_id=(g, i, t), device_id_type=MESH)

    def heads_from(k, piece):
        return pltpu.make_async_remote_copy(
            heads(1, piece), here(k, piece), gsend.at[piece, 0], grecv.at[piece, k],
            device_id=(g, near, t), device_id_type=MESH)

    def heads_own(i, piece):
        return pltpu.make_async_copy(heads(i, piece), here(i, piece), hsem.at[piece])

    def pass_on(src, k):
        return pltpu.make_async_remote_copy(
            src, given.at[pl.ds(k * tokens, tokens), 2 * strip:3 * strip], fsend.at[k], frecv.at[k],
            device_id=(g, z, across), device_id_type=MESH)

    def pass_on_from(k):
        @pl.when(inner)
        def _():
            heads_from(k, 0).wait_recv()
            pass_on(here(k, 0), k).start()

    for i in range(7):
        table_to(i).start()
    for i in (1, 2):
        @pl.when(z == i)
        def _():
            for piece in range(2):
                heads_to(3 - i, piece).start()
                heads_own(i, piece).start()
            pass_on(heads(i, 0), i).start()

        @pl.when(z == 6 - 3 * i)
        def _():
            heads_to(i, 0).start()
            heads_to(3 - i, 0).start()
            heads_to(i, 1).start()
    tables[z] = table[...]

    step = 8
    for i in range(fetches):
        fetch(i).wait()

        def squares(b, carry):
            first = pl.multiple_of(i * per + b * step, step)
            for tap in range(taps):
                total = jnp.zeros((step, block, LANES), jnp.float32)
                for c in range(chunks):
                    x = xbuf[pl.ds(first, step), tap, :, c * LANES:(c + 1) * LANES].astype(jnp.float32)
                    total = total + x * x
                psq[tap, pl.ds(pl.multiple_of(first * block, step * block), step * block), :] = total.reshape(
                    step * block, LANES)
            return carry

        lax.fori_loop(0, per // step, squares, 0)
    sums[0] = jnp.zeros((8, tokens), jnp.float32)
    for tap in range(taps):
        sums[0, tap:tap + 1, :] = jnp.sum(psq[tap].T, axis=0, keepdims=True)

    def sums_to(k):
        return pltpu.make_async_remote_copy(
            sums.at[0], sums.at[k], ssend.at[k - 1], srecv.at[k - 1],
            device_id=(g, z, lax.rem(t + k, 4)), device_id_type=MESH)

    for k in range(1, 4):
        sums_to(k).start()

    for k in range(1, 4):
        table_from(lax.rem(z + k, 4)).wait_recv()
    for k in range(4):
        table_from(4 + k).wait_recv()
    for k in range(8):
        index = (tables[k, 0:1, :] * owned + tables[k, 1:2, :]).astype(jnp.float32)
        columns_of[k, 0] = jnp.broadcast_to(index, (LANES, LANES)).T[0:owned]
        columns_of[k, 1] = jnp.broadcast_to(tables[k, 2:3, :].astype(jnp.float32), (LANES, LANES)).T[0:owned]

    def most_of(r, at):
        most = jnp.zeros((owned, LANES), jnp.float32)
        for k in range(4):
            most = jnp.maximum(most, jnp.where(columns_of[4 * r + k, 0] == at, columns_of[4 * r + k, 1], 0.0))
        return jnp.max(most, axis=0, keepdims=True)

    blocks = 4 * owned
    most = jnp.concatenate([
        most_of(0, (n * LANES + lax.broadcasted_iota(jnp.int32, (1, LANES), 1)).astype(jnp.float32))
        for n in range(blocks // LANES)], axis=1)
    most = jnp.broadcast_to(most, (8, blocks)).astype(jnp.bfloat16)
    token = lax.broadcasted_iota(jnp.int32, (LANES, tokens), 1)
    spread = jnp.where(
        lax.div(token, block) == lax.broadcasted_iota(jnp.int32, (LANES, tokens), 0), 1.0, 0.0).astype(jnp.bfloat16)
    offset = lax.rem(lax.broadcasted_iota(jnp.int32, (1, tokens), 1), block)
    for k in range(4):
        index = tables[k, 0:1, :] * owned + tables[k, 1:2, :]
        other = lax.broadcasted_iota(jnp.int32, (blocks, LANES), 0)
        ahead_of = jnp.where(
            jnp.logical_and(other < index, other >= jnp.where(index < blocks // 2, 0, blocks // 2)), 1.0, 0.0)
        rows_ahead = jnp.dot(most, ahead_of.astype(jnp.bfloat16), preferred_element_type=jnp.float32)[0:1].astype(jnp.int32)
        high = lax.div(rows_ahead, 64)
        entry = jnp.concatenate(
            [tables[k, 0:3, :], high, rows_ahead - 64 * high, jnp.zeros((3, LANES), jnp.int32)], axis=0)
        entry = jnp.dot(
            entry.astype(jnp.float32).astype(jnp.bfloat16), spread, preferred_element_type=jnp.float32
        ).astype(jnp.int32)
        alive = offset < entry[2:3]
        row = (entry[0:1] * owned + entry[1:2]) * block + offset
        names[k] = jnp.broadcast_to(jnp.where(alive, row, -1), (8, tokens))
        within = entry[3:4] * 64 + entry[4:5] + offset
        alive = jnp.logical_and(alive, within < limit)
        places[k] = jnp.broadcast_to(
            jnp.where(alive, within + jnp.where(entry[0:1] < 2, 0, limit), -1), (8, tokens))
    row_chunks = 4 * tokens // LANES

    def mark(c, carry):
        row = c * LANES + lax.broadcasted_iota(jnp.int32, (1, LANES), 1)
        at = lax.div(row, block).astype(jnp.float32)
        for r in range(2):
            most = most_of(r, at)
            used[r, pl.ds(c, 1), :] = jnp.where(lax.rem(row, block).astype(jnp.float32) < most, 1.0, 0.0)
        return carry

    lax.fori_loop(0, row_chunks, mark, 0)
    before = jnp.where(
        lax.broadcasted_iota(jnp.int32, (LANES, LANES), 0) < lax.broadcasted_iota(jnp.int32, (LANES, LANES), 1),
        1.0, 0.0).astype(jnp.bfloat16)
    excess = jnp.full((1, LANES), -1.0, jnp.float32)
    zero = jnp.zeros((1, LANES), jnp.float32)
    for r in range(2):
        local = jnp.dot(used[r].astype(jnp.bfloat16), before, preferred_element_type=jnp.float32)
        for c in range(row_chunks):
            if c % (row_chunks // 2) == 0:
                base = zero
            if c % (row_chunks // 4) == 0:
                run = zero
            flags = used[r, c:c + 1, :]
            if r == 0:
                rank = jnp.where(flags > 0.0, local[c:c + 1] + run, -1.0)
                at = slice(c * LANES, (c + 1) * LANES)
                ranks[0, :, at] = jnp.broadcast_to(jnp.where(flags > 0.0, rank + base, -1.0).astype(jnp.int32), (8, LANES))
                ranks[1, :, at] = jnp.broadcast_to(rank.astype(jnp.int32), (8, LANES))
            run = run + jnp.broadcast_to(jnp.sum(flags, axis=1, keepdims=True), (1, LANES))
            if (c + 1) % (row_chunks // 4) == 0:
                which = c // (row_chunks // 4)
                if r == 0:
                    counts[which] = jnp.broadcast_to(run.astype(jnp.int32), (8, LANES))
                if which in (0, 3):
                    excess = jnp.maximum(excess, run - float(room))
                base = base + run
                excess = jnp.maximum(excess, base - float(limit))
    unfit[0, 0] = jnp.max(excess).astype(jnp.int32)

    def one_hot(to, count, row):
        def some(n, carry):
            first = pl.multiple_of(n * 64, 64)
            at = first + lax.broadcasted_iota(jnp.int32, (64, row.shape[1]), 0)
            to[pl.ds(first, 64), :] = jnp.where(row == at, 1.0, 0.0).astype(jnp.bfloat16)
            return carry

        lax.fori_loop(0, count // 64, some, 0)

    own_rows = pl.ds(pl.multiple_of(z * tokens, tokens), tokens)

    @pl.when(outer)
    def _():
        one_hot(outer_pick, room, ranks[1, 0:1, own_rows])

    pass_on_from(edge)
    for k in range(1, 4):
        sums_to(k).wait()
    inverse = lax.rsqrt((sums[0] + sums[1] + sums[2] + sums[3]) / width + EPSILON)
    for tap in range(taps):
        invb[tap] = jnp.broadcast_to(inverse[tap:tap + 1, :], (LANES, tokens)).T
    gains.wait()

    def store(c):
        return pltpu.make_async_copy(pair.at[c, 0:tokens], united.at[c], osem.at[c])

    def rows_to(c):
        return pltpu.make_async_remote_copy(
            packed.at[c, 0:room], pair.at[c, tokens:tokens + room], nsend.at[c], nrecv.at[c],
            device_id=(g, near, t), device_id_type=MESH)

    def unite(c, carry):
        lanes = pl.ds(pl.multiple_of(c * LANES, LANES), LANES)
        scale = [gain[tap:tap + 1, lanes] for tap in range(taps)]
        for b in range(owned // step):
            total = jnp.zeros((step * block, LANES), jnp.float32)
            for tap in range(taps):
                x = xbuf[b * step:(b + 1) * step, tap, :, lanes].astype(jnp.float32).reshape(step * block, LANES)
                total = total + x * invb[tap, b * step * block:(b + 1) * step * block, :] * scale[tap]
            pair[c, b * step * block:(b + 1) * step * block, :] = total.astype(jnp.bfloat16)
        store(c).start()

        @pl.when(outer)
        def _():
            packed[c, 0:room, :] = jnp.dot(
                outer_pick[...], pair[c, 0:tokens, :], preferred_element_type=jnp.float32).astype(jnp.bfloat16)
            rows_to(c).start()

        return carry

    lax.fori_loop(0, 1, unite, 0)
    for i in (1, 2):
        @pl.when(z == 3 * i - 3)
        def _():
            heads_to(i, 1).start()

    lax.fori_loop(1, chunks // 2, unite, 0)
    pass_on_from(partner)
    lax.fori_loop(chunks // 2, chunks, unite, 0)
    pass_on_from(beyond)

    part = 2 * strip
    side = z - 1
    beside = t + 1 - 2 * lax.rem(t, 2)
    opposite = lax.rem(beside + 2, 4)

    def packed_to(c, which):
        here = packed.at[c, pl.ds(which * limit, limit)]
        return pltpu.make_async_remote_copy(
            here, here, psend.at[c], precv.at[c], device_id=(g, partner, t), device_id_type=MESH)

    def slots_to(row, piece, to, sem):
        here = slots.at[piece, pl.ds(row * strip, strip)]
        return pltpu.make_async_remote_copy(
            here, here, asend.at[sem + piece], arecv.at[sem + piece], device_id=(g, z, to), device_id_type=MESH)

    def back(c, piece, to):
        here = cbuf.at[c, piece]
        return pltpu.make_async_remote_copy(
            here, here, csend.at[piece, c], crecv.at[piece, c], device_id=(g, to, t), device_id_type=MESH)

    def back_whole(c, to):
        here = cbuf.at[c]
        return pltpu.make_async_remote_copy(
            here, here, csend.at[0, c], crecv.at[0, c], device_id=(g, to, t), device_id_type=MESH)

    @pl.when(inner)
    def _():
        outer_rank = lax.broadcasted_iota(jnp.int32, (1, room), 1)
        outer_count = jnp.concatenate([counts[edge, 0:1, :]] * (room // LANES), axis=1)
        outer_base = jnp.concatenate([jnp.where(z == 1, 0, counts[2, 0:1, :])] * (room // LANES), axis=1)
        one_hot(pair_pick, limit, jnp.concatenate([
            ranks[0, 0:1, own_rows], jnp.where(outer_rank < outer_count, outer_rank + outer_base, -1)], axis=1))

        def choose(n, carry):
            first = pl.multiple_of(n * 64, 64)
            at = first + lax.broadcasted_iota(jnp.int32, (64, tokens), 0)
            for k in range(4):
                chosen[pl.ds(first, 64), k * tokens:(k + 1) * tokens] = jnp.where(
                    places[k, 0:1, :] == at, 1.0, 0.0).astype(jnp.bfloat16)
            return carry

        lax.fori_loop(0, 2 * limit // 64, choose, 0)

        def strip_of(piece, row):
            return piece, pl.ds(pl.multiple_of(row * strip, strip), strip)

        def heads_arrive(piece):
            for i in (1, 2):
                @pl.when(z == i)
                def _():
                    heads_own(i, piece).wait()
                    for k in range(4):
                        if piece == 0:
                            pass_on(here(k, 0), k).wait()
                        elif k != i:
                            heads_from(k, 1).wait_recv()

        def sum_first(n, carry):
            rows = pl.ds(pl.multiple_of(n * 384, 384), 384)
            some = jnp.dot(chosen[rows, :], given[:, strip:3 * strip], preferred_element_type=jnp.float32)
            some = some.T.astype(jnp.bfloat16)
            slots[(*strip_of(0, t), rows)] = some[0:strip]
            slots[(*strip_of(0, across), rows)] = some[strip:2 * strip]
            return carry

        def sum_second(n, carry):
            rows = pl.ds(pl.multiple_of(n * 384, 384), 384)
            some = jnp.dot(chosen[rows, :], given[:, 0:strip], preferred_element_type=jnp.float32)
            slots[(*strip_of(1, t), rows)] = some.T.astype(jnp.bfloat16)
            return carry

        def pack(c):
            rows_to(c).wait_recv()
            few = jnp.dot(pair_pick[...], pair[c], preferred_element_type=jnp.float32)
            packed[c, pl.ds(pl.multiple_of(side * limit, limit), limit), :] = few.astype(jnp.bfloat16)
            packed_to(c, side).start()

        mine = pl.multiple_of(jnp.where(z == 1, part, 0), part)
        theirs = pl.multiple_of(part - mine, part)

        def send_back(c, piece, go=True):
            cbuf[c, piece] = jnp.dot(
                slots[piece, pl.ds(theirs, part), :], packed[c], preferred_element_type=jnp.float32
            ).astype(jnp.bfloat16)
            if go:
                back(c, piece, edge).start()

        def keep(c):
            lanes = pl.ds(pl.multiple_of(c * LANES, LANES), LANES)
            for piece in range(2):
                rows = jnp.dot(
                    slots[piece, pl.ds(mine, part), :], packed[c], preferred_element_type=jnp.float32)
                for which in range(2):
                    first = which * part + piece * strip
                    out[first:first + strip, lanes] = rows[which * strip:(which + 1) * strip]

        def gathered(piece):
            if piece == 1:
                slots_to(across, piece, across, 0).wait_recv()
                slots_to(across, piece, beside, 4).start()
            slots_to(beside, piece, beside, 2).wait_recv()
            slots_to(opposite, piece, beside, 4).wait_recv()

        pack(0)
        heads_arrive(0)
        lax.fori_loop(0, 2 * limit // 384, sum_first, 0)
        slots_to(t, 0, beside, 2).start()
        slots_to(across, 0, beside, 4).start()
        pack(1)
        heads_arrive(1)
        given_copy = pltpu.make_async_copy(given, given_out, dsem.at[0])
        given_copy.start()
        lax.fori_loop(0, 2 * limit // 384, sum_second, 0)
        slots_to(t, 1, across, 0).start()
        slots_to(t, 1, beside, 2).start()

        early, ahead = 1, 4
        pack(2)
        pack(3)
        gathered(0)
        for c in range(early):
            packed_to(c, 1 - side).wait_recv()
            send_back(c, 0)
            pack(c + ahead)
        gathered(1)
        for c in range(early):
            send_back(c, 1)

        def product(c, carry):
            packed_to(c, 1 - side).wait_recv()
            for piece in range(2):
                send_back(c, piece, False)
            back_whole(c, edge).start()

            @pl.when(c + ahead < chunks)
            def _():
                pack(c + ahead)

            keep(c - early)
            return carry

        lax.fori_loop(early, chunks, product, 0)

        def last(c, carry):
            keep(c)
            return carry

        lax.fori_loop(chunks - early, chunks, last, 0)

        def sent(c, carry):
            packed_to(c, side).wait_send()
            return carry

        lax.fori_loop(0, chunks, sent, 0)
        for c in range(early):
            for piece in range(2):
                back(c, piece, edge).wait_send()

        def sent_whole(c, carry):
            back_whole(c, edge).wait_send()
            return carry

        lax.fori_loop(early, chunks, sent_whole, 0)
        given_copy.wait()
        slots_to(t, 1, across, 0).wait_send()
        for piece in range(2):
            slots_to(t, piece, beside, 2).wait_send()
            slots_to(across, piece, beside, 4).wait_send()

    @pl.when(outer)
    def _():
        def place_rows(c, piece):
            lanes = pl.ds(pl.multiple_of(c * LANES, LANES), LANES)
            for which in range(2):
                first = which * part + piece * strip
                out[first:first + strip, lanes] = cbuf[c, piece, which * strip:(which + 1) * strip].astype(jnp.float32)

        for c in range(1):
            for piece in range(2):
                back(c, piece, near).wait_recv()
                place_rows(c, piece)

        def arrive(c, carry):
            back_whole(c, near).wait_recv()
            for piece in range(2):
                place_rows(c, piece)
            return carry

        lax.fori_loop(1, chunks, arrive, 0)

        def sent(c, carry):
            rows_to(c).wait_send()
            return carry

        lax.fori_loop(0, chunks, sent, 0)

    def stored(c, carry):
        store(c).wait()
        return carry

    lax.fori_loop(0, chunks, stored, 0)
    for i in (1, 2):
        @pl.when(z != i)
        def _():
            for piece in range(2):
                heads_to(i, piece).wait_send()
    for i in range(7):
        table_to(i).wait_send()


def whole_kernel(
    united, given, names, out,
    everywhere, slots, cbuf,
    lsem, usend, urecv, asend, arecv, csend, crecv,
):
    g, z, t = place()
    chunks, tokens, _ = united.shape
    strip = given.shape[1] // 3
    part = 2 * strip
    half = 2 * part
    inner = jnp.logical_or(z == 1, z == 2)
    outer = jnp.logical_not(inner)
    partner = 3 - z
    near = jnp.where(z < 2, 1, 2)
    far = 3 - near
    edge = jnp.where(z == 1, 0, 3)
    beyond = 3 - edge
    across = lax.rem(t + 2, 4)
    beside = t + 1 - 2 * lax.rem(t, 2)
    opposite = lax.rem(beside + 2, 4)
    barrier = pltpu.get_barrier_semaphore()

    def rows_to(c, to, sem):
        return pltpu.make_async_remote_copy(
            united.at[c], everywhere.at[c, pl.ds(z * tokens, tokens)], usend.at[sem, c], urecv.at[z, c],
            device_id=(g, to, t), device_id_type=MESH)

    def rows_from(c, k):
        return pltpu.make_async_remote_copy(
            united.at[c], everywhere.at[c, pl.ds(k * tokens, tokens)], usend.at[0, c], urecv.at[k, c],
            device_id=(g, partner, t), device_id_type=MESH)

    def slots_to(row, to, sem):
        here = slots.at[pl.ds(row * part, part)]
        return pltpu.make_async_remote_copy(
            here, here, asend.at[sem], arecv.at[sem], device_id=(g, z, to), device_id_type=MESH)

    def back(c, to):
        return pltpu.make_async_remote_copy(
            cbuf.at[c], cbuf.at[c], csend.at[c], crecv.at[c], device_id=(g, to, t), device_id_type=MESH)

    @pl.when(inner)
    def _():
        own = pltpu.make_async_copy(united, everywhere.at[:, pl.ds(z * tokens, tokens)], lsem.at[0])
        own.start()
        signal_all(barrier, [(g, partner, t), (g, edge, t), (g, beyond, t), (g, z, across), (g, z, beside)])
        pl.semaphore_wait(barrier, 5)

        def give(c, carry):
            rows_to(c, partner, 0).start()
            return carry

        lax.fori_loop(0, chunks, give, 0)

        def some_rows(j, carry):
            first = pl.multiple_of(j * 256, 256)
            total = sum_by_row(names, given, first, tokens).T.astype(jnp.bfloat16)
            for piece in range(2):
                slots[pl.ds(pl.multiple_of(t * part + piece * strip, strip), strip), pl.ds(first, 256)] = total[
                    (1 - piece) * strip:(2 - piece) * strip]
            return carry

        lax.fori_loop(0, 4 * tokens // 256, some_rows, 0)
        slots_to(t, across, 0).start()
        slots_to(t, beside, 1).start()
        own.wait()
        slots_to(across, across, 0).wait_recv()
        slots_to(across, beside, 2).start()
        slots_to(beside, beside, 1).wait_recv()
        slots_to(opposite, beside, 2).wait_recv()

        mine = pl.multiple_of(jnp.where(z == 1, half, 0), half)
        theirs = pl.multiple_of(half - mine, half)

        def product(c, carry):
            for k in range(4):
                @pl.when(z != k)
                def _():
                    rows_from(c, k).wait_recv()
            rows = everywhere[c]
            cbuf[c] = jnp.dot(
                slots[pl.ds(theirs, half), :], rows, preferred_element_type=jnp.float32).astype(jnp.bfloat16)
            back(c, edge).start()
            lanes = pl.ds(pl.multiple_of(c * LANES, LANES), LANES)
            out[:, lanes] = jnp.dot(
                slots[pl.ds(mine, half), :], rows, preferred_element_type=jnp.float32)
            return carry

        lax.fori_loop(0, chunks, product, 0)

        def sent(c, carry):
            rows_to(c, partner, 0).wait_send()
            back(c, edge).wait_send()
            return carry

        lax.fori_loop(0, chunks, sent, 0)
        slots_to(t, across, 0).wait_send()
        slots_to(t, beside, 1).wait_send()
        slots_to(across, beside, 2).wait_send()

    @pl.when(outer)
    def _():
        signal_all(barrier, [(g, near, t), (g, far, t)])
        pl.semaphore_wait(barrier, 2)

        def give(c, carry):
            rows_to(c, far, 0).start()
            rows_to(c, near, 1).start()
            return carry

        lax.fori_loop(0, chunks, give, 0)

        def arrive(c, carry):
            back(c, near).wait_recv()
            lanes = pl.ds(pl.multiple_of(c * LANES, LANES), LANES)
            out[:, lanes] = cbuf[c].astype(jnp.float32)
            return carry

        lax.fori_loop(0, chunks, arrive, 0)

        def sent(c, carry):
            rows_to(c, far, 0).wait_send()
            rows_to(c, near, 1).wait_send()
            return carry

        lax.fori_loop(0, chunks, sent, 0)


def line_body(feature_cache, owner_ids, slot_ids, live_tokens, tap_gain, key_cotangent, value_cotangent):
    owned, block, taps, columns = feature_cache.shape
    tokens = owned * block
    part = key_cotangent.shape[1]
    chunks = columns // LANES
    vmem, hbm = pl.BlockSpec(memory_space=pltpu.VMEM), pl.BlockSpec(memory_space=pltpu.HBM)
    dma = pltpu.SemaphoreType.DMA
    shape = jax.ShapeDtypeStruct

    def params(number, mebibytes):
        return pltpu.CompilerParams(
            collective_id=number, has_side_effects=True, vmem_limit_bytes=mebibytes * 2**20)

    room, limit = 3 * tokens // 4, 9 * tokens // 8
    shapes = (
        shape((2 * part, columns), jnp.float32),
        shape((chunks, tokens, LANES), jnp.bfloat16),
        shape((4 * tokens, part + part // 2), jnp.bfloat16),
        shape((4, 8, tokens), jnp.int32),
        shape((1, 1), jnp.int32),
    )
    gradient, united, given, names, unfit = pl.pallas_call(
        packed_kernel,
        out_shape=shapes,
        in_specs=[hbm] * 7,
        out_specs=(vmem, hbm, hbm, vmem, pl.BlockSpec(memory_space=pltpu.SMEM)),
        scratch_shapes=[
            pltpu.VMEM((4 * tokens, part + part // 2), jnp.bfloat16),
            pltpu.VMEM((owned, taps, block, columns), jnp.bfloat16),
            pltpu.VMEM((taps, columns), jnp.float32),
            pltpu.VMEM((3, 1, owned), jnp.int32),
            pltpu.VMEM((8, LANES), jnp.int32),
            pltpu.VMEM((8, 8, LANES), jnp.int32),
            pltpu.VMEM((8, 2, owned, LANES), jnp.float32),
            pltpu.VMEM((2, 4 * tokens // LANES, LANES), jnp.float32),
            pltpu.VMEM((2, 8, 4 * tokens), jnp.int32),
            pltpu.VMEM((4, 8, LANES), jnp.int32),
            pltpu.VMEM((taps, tokens, LANES), jnp.float32),
            pltpu.VMEM((4, 8, tokens), jnp.float32),
            pltpu.VMEM((taps, tokens, LANES), jnp.float32),
            pltpu.VMEM((chunks, tokens + room, LANES), jnp.bfloat16),
            pltpu.VMEM((2 * limit, 4 * tokens), jnp.bfloat16),
            pltpu.VMEM((limit, tokens + room), jnp.bfloat16),
            pltpu.VMEM((room, tokens), jnp.bfloat16),
            pltpu.VMEM((4, 8, tokens), jnp.int32),
            pltpu.VMEM((chunks, 2 * limit, LANES), jnp.bfloat16),
            pltpu.VMEM((2, 2 * part, 2 * limit), jnp.bfloat16),
            pltpu.VMEM((chunks, 2, part, LANES), jnp.bfloat16),
            dma((4,)), dma((4,)),
            dma((7,)), dma((8,)),
            dma((2, 2)), dma((2, 4)), dma((2,)),
            dma((4,)), dma((4,)),
            dma((3,)), dma((3,)),
            dma((chunks,)), dma((1,)),
            dma((chunks,)), dma((chunks,)),
            dma((chunks,)), dma((chunks,)),
            dma((6,)), dma((6,)),
            dma((2, chunks)), dma((2, chunks)),
        ],
        compiler_params=params(0, 58),
    )(
        jnp.transpose(feature_cache, (0, 2, 1, 3)), owner_ids.reshape(1, owned), slot_ids.reshape(1, owned),
        live_tokens.reshape(1, owned), tap_gain, key_cotangent, value_cotangent)

    def whole(_, *given):
        return pl.pallas_call(
            whole_kernel,
            out_shape=shapes[0],
            in_specs=[hbm, vmem, vmem],
            out_specs=vmem,
            scratch_shapes=[
                pltpu.VMEM((chunks, 4 * tokens, LANES), jnp.bfloat16),
                pltpu.VMEM((4 * part, 4 * tokens), jnp.bfloat16),
                pltpu.VMEM((chunks, 2 * part, LANES), jnp.bfloat16),
                dma((1,)),
                dma((2, chunks)), dma((4, chunks)),
                dma((3,)), dma((3,)),
                dma((chunks,)), dma((chunks,)),
            ],
            compiler_params=params(1, 40),
        )(*given)

    def fits(gradient, *_):
        return gradient

    return lax.cond(unfit[0, 0] <= 0, fits, whole, gradient, united, given, names)


def solution(mesh):
    in_specs = (
        P(("groups", "dp"), None, None, "tensor"),
        P(("groups", "dp"), None),
        P(("groups", "dp")),
        P(("groups", "dp")),
        P(None, "tensor"),
        P(("groups", "dp"), "tensor"),
        P(("groups", "dp"), "tensor"),
    )
    out_specs = P(("groups", "dp"), "tensor")
    line = tuple(mesh.shape[axis] for axis in ("groups", "dp", "tensor")) == (2, 4, 4)
    body = line_body if line else gather_body
    return jax.shard_map(body, mesh=mesh, in_specs=in_specs, out_specs=out_specs, check_vma=False)
```

```python
import functools

import jax
import jax.numpy as jnp
from jax import lax
from jax.experimental import pallas as pl
from jax.experimental.pallas import tpu as pltpu
from jax.sharding import PartitionSpec as P

EPSILON = 1e-06
MESH = pl.DeviceIdType.MESH
LANES = 128


def united_of(feature_cache, tap_gain, width):
    floats = feature_cache.astype(jnp.float32)
    squares = lax.psum(jnp.sum(floats * floats, axis=-1), "tensor")
    inverse_rms = lax.rsqrt(squares / width + EPSILON)
    return jnp.sum(floats * inverse_rms[..., None] * tap_gain, axis=2).astype(jnp.bfloat16)


def slot_matrix(owner_ids, slot_ids, live_tokens, owned, dtype):
    index = owner_ids[:, 0] * owned + slot_ids
    table = lax.all_gather(jnp.stack([index, live_tokens]), "dp", axis=1, tiled=True)
    slots = lax.axis_size("dp") * owned
    chosen = jnp.arange(slots, dtype=jnp.int32)[:, None] == table[0][None, :]
    return chosen.astype(dtype), table[1]


def gather_body(feature_cache, owner_ids, slot_ids, live_tokens, tap_gain, key_cotangent, value_cotangent):
    owned, block_len, _, columns = feature_cache.shape
    width = columns * lax.axis_size("tensor")
    united = united_of(feature_cache, tap_gain, width).reshape(owned * block_len, columns)
    everywhere = lax.all_gather(united, "dp", axis=0, tiled=True)
    chosen, live = slot_matrix(owner_ids, slot_ids, live_tokens, owned, jnp.bfloat16)
    joined = jnp.concatenate(
        [
            lax.all_gather(key_cotangent, "tensor", axis=1, tiled=True),
            lax.all_gather(value_cotangent, "tensor", axis=1, tiled=True),
        ],
        axis=1,
    )
    mine = lax.all_to_all(joined, "dp", split_axis=1, concat_axis=0, tiled=True)
    rows = mine.shape[1]
    mine = mine.reshape(-1, block_len, rows)
    mask = jnp.arange(block_len, dtype=jnp.int32)[None, :] < live[:, None]
    mine = jnp.where(mask[:, :, None], mine, jnp.zeros_like(mine)).reshape(-1, block_len * rows)
    by_slot = lax.dot_general(
        chosen, mine, (((1,), (0,)), ((), ())), preferred_element_type=jnp.float32
    ).astype(jnp.bfloat16).reshape(-1, rows)
    return lax.dot_general(
        by_slot, everywhere, (((0,), (0,)), ((), ())), preferred_element_type=jnp.float32
    )


def place():
    return tuple(lax.axis_index(n) for n in ("groups", "dp", "tensor"))


def signal_all(barrier, ids):
    for to in ids:
        pl.semaphore_signal(barrier, inc=1, device_id=to, device_id_type=MESH)


def sum_by_row(names, given, first, tokens):
    at = first + lax.broadcasted_iota(jnp.int32, (256, tokens), 0)
    total = jnp.zeros((256, given.shape[1]), jnp.float32)
    for k in range(4):
        chosen = jnp.where(names[k, 0:1, :] == at, 1.0, 0.0).astype(jnp.bfloat16)
        total = total + jnp.dot(chosen, given[k * tokens:(k + 1) * tokens, :], preferred_element_type=jnp.float32)
    return total


def packed_kernel(
    feats, owner, slot, live, gain_in, key, value,
    out, united, given_out, names, unfit,
    given, xbuf, gain, lists, table, tables, columns_of, used, ranks, counts, psq, sums, invb,
    pair, chosen, pair_pick, outer_pick, places, packed, slots, cbuf,
    xsem, lsem, bsend, brecv, gsend, grecv, hsem, fsend, frecv, ssend, srecv, osem, dsem,
    nsend, nrecv, psend, precv, asend, arecv, csend, crecv,
):
    g, z, t = place()
    owned, taps, block, columns = feats.shape
    tokens = owned * block
    chunks = columns // LANES
    width = columns * 4
    inner = jnp.logical_or(z == 1, z == 2)
    outer = jnp.logical_not(inner)
    room = outer_pick.shape[0]
    limit = pair_pick.shape[0]
    near = jnp.where(z < 2, 1, 2)
    fetches = 4
    per = owned // fetches

    def fetch(i):
        return pltpu.make_async_copy(feats.at[pl.ds(i * per, per)], xbuf.at[pl.ds(i * per, per)], xsem.at[i])

    small = [pltpu.make_async_copy(src, lists.at[i], lsem.at[i]) for i, src in enumerate((owner, slot, live))]
    for copy in small:
        copy.start()
    for i in range(fetches):
        fetch(i).start()
    gains = pltpu.make_async_copy(gain_in, gain, lsem.at[3])
    gains.start()

    barrier = pltpu.get_barrier_semaphore()
    others = [(g, lax.rem(z + k, 4), t) for k in range(1, 4)] + [(1 - g, lax.rem(z + k, 4), t) for k in range(4)]
    signal_all(barrier, others + [(g, z, lax.rem(t + k, 4)) for k in range(1, 4)])
    table[...] = jnp.zeros(table.shape, jnp.int32)
    for i, copy in enumerate(small):
        copy.wait()
        table[i:i + 1, 0:owned] = lists[i]
    pl.semaphore_wait(barrier, 10)

    def table_to(i):
        at = z if i < 3 else 4 + z
        return pltpu.make_async_remote_copy(
            table, tables.at[at], bsend.at[i], brecv.at[at], device_id=others[i], device_id_type=MESH)

    def table_from(at):
        return pltpu.make_async_remote_copy(
            table, tables.at[at], bsend.at[0], brecv.at[at], device_id=others[0], device_id_type=MESH)

    strip = key.shape[1] // 2
    across = lax.rem(t + 2, 4)
    edge = jnp.where(z == 1, 0, 3)
    partner, beyond = 3 - z, 3 - edge

    def heads(i, piece):
        return (key if i == 1 else value).at[:, piece * strip:(piece + 1) * strip]

    def here(k, piece):
        return given.at[pl.ds(k * tokens, tokens), (1 - piece) * strip:(2 - piece) * strip]

    def heads_to(i, piece):
        return pltpu.make_async_remote_copy(
            heads(i, piece), here(z, piece), gsend.at[piece, i - 1], grecv.at[piece, z],
            device_id=(g, i, t), device_id_type=MESH)

    def heads_from(k, piece):
        return pltpu.make_async_remote_copy(
            heads(1, piece), here(k, piece), gsend.at[piece, 0], grecv.at[piece, k],
            device_id=(g, near, t), device_id_type=MESH)

    def heads_own(i, piece):
        return pltpu.make_async_copy(heads(i, piece), here(i, piece), hsem.at[piece])

    def pass_on(src, k):
        return pltpu.make_async_remote_copy(
            src, given.at[pl.ds(k * tokens, tokens), 2 * strip:3 * strip], fsend.at[k], frecv.at[k],
            device_id=(g, z, across), device_id_type=MESH)

    def pass_on_from(k):
        @pl.when(inner)
        def _():
            heads_from(k, 0).wait_recv()
            pass_on(here(k, 0), k).start()

    for i in range(7):
        table_to(i).start()
    for i in (1, 2):
        @pl.when(z == i)
        def _():
            for piece in range(2):
                heads_to(3 - i, piece).start()
                heads_own(i, piece).start()
            pass_on(heads(i, 0), i).start()

        @pl.when(z == 6 - 3 * i)
        def _():
            heads_to(i, 0).start()
            heads_to(3 - i, 0).start()
            heads_to(i, 1).start()
    tables[z] = table[...]

    step = 8
    for i in range(fetches):
        fetch(i).wait()

        def squares(b, carry):
            first = pl.multiple_of(i * per + b * step, step)
            for tap in range(taps):
                total = jnp.zeros((step, block, LANES), jnp.float32)
                for c in range(chunks):
                    x = xbuf[pl.ds(first, step), tap, :, c * LANES:(c + 1) * LANES].astype(jnp.float32)
                    total = total + x * x
                psq[tap, pl.ds(pl.multiple_of(first * block, step * block), step * block), :] = total.reshape(
                    step * block, LANES)
            return carry

        lax.fori_loop(0, per // step, squares, 0)
    sums[0] = jnp.zeros((8, tokens), jnp.float32)
    for tap in range(taps):
        sums[0, tap:tap + 1, :] = jnp.sum(psq[tap].T, axis=0, keepdims=True)

    def sums_to(k):
        return pltpu.make_async_remote_copy(
            sums.at[0], sums.at[k], ssend.at[k - 1], srecv.at[k - 1],
            device_id=(g, z, lax.rem(t + k, 4)), device_id_type=MESH)

    for k in range(1, 4):
        sums_to(k).start()

    for k in range(1, 4):
        table_from(lax.rem(z + k, 4)).wait_recv()
    for k in range(4):
        table_from(4 + k).wait_recv()
    for k in range(8):
        index = (tables[k, 0:1, :] * owned + tables[k, 1:2, :]).astype(jnp.float32)
        columns_of[k, 0] = jnp.broadcast_to(index, (LANES, LANES)).T[0:owned]
        columns_of[k, 1] = jnp.broadcast_to(tables[k, 2:3, :].astype(jnp.float32), (LANES, LANES)).T[0:owned]

    def most_of(r, at):
        most = jnp.zeros((owned, LANES), jnp.float32)
        for k in range(4):
            most = jnp.maximum(most, jnp.where(columns_of[4 * r + k, 0] == at, columns_of[4 * r + k, 1], 0.0))
        return jnp.max(most, axis=0, keepdims=True)

    blocks = 4 * owned
    most = jnp.concatenate([
        most_of(0, (n * LANES + lax.broadcasted_iota(jnp.int32, (1, LANES), 1)).astype(jnp.float32))
        for n in range(blocks // LANES)], axis=1)
    most = jnp.broadcast_to(most, (8, blocks)).astype(jnp.bfloat16)
    token = lax.broadcasted_iota(jnp.int32, (LANES, tokens), 1)
    spread = jnp.where(
        lax.div(token, block) == lax.broadcasted_iota(jnp.int32, (LANES, tokens), 0), 1.0, 0.0).astype(jnp.bfloat16)
    offset = lax.rem(lax.broadcasted_iota(jnp.int32, (1, tokens), 1), block)
    for k in range(4):
        index = tables[k, 0:1, :] * owned + tables[k, 1:2, :]
        other = lax.broadcasted_iota(jnp.int32, (blocks, LANES), 0)
        ahead_of = jnp.where(
            jnp.logical_and(other < index, other >= jnp.where(index < blocks // 2, 0, blocks // 2)), 1.0, 0.0)
        rows_ahead = jnp.dot(most, ahead_of.astype(jnp.bfloat16), preferred_element_type=jnp.float32)[0:1].astype(jnp.int32)
        high = lax.div(rows_ahead, 64)
        entry = jnp.concatenate(
            [tables[k, 0:3, :], high, rows_ahead - 64 * high, jnp.zeros((3, LANES), jnp.int32)], axis=0)
        entry = jnp.dot(
            entry.astype(jnp.float32).astype(jnp.bfloat16), spread, preferred_element_type=jnp.float32
        ).astype(jnp.int32)
        alive = offset < entry[2:3]
        row = (entry[0:1] * owned + entry[1:2]) * block + offset
        names[k] = jnp.broadcast_to(jnp.where(alive, row, -1), (8, tokens))
        within = entry[3:4] * 64 + entry[4:5] + offset
        alive = jnp.logical_and(alive, within < limit)
        places[k] = jnp.broadcast_to(
            jnp.where(alive, within + jnp.where(entry[0:1] < 2, 0, limit), -1), (8, tokens))
    row_chunks = 4 * tokens // LANES

    def mark(c, carry):
        row = c * LANES + lax.broadcasted_iota(jnp.int32, (1, LANES), 1)
        at = lax.div(row, block).astype(jnp.float32)
        for r in range(2):
            most = most_of(r, at)
            used[r, pl.ds(c, 1), :] = jnp.where(lax.rem(row, block).astype(jnp.float32) < most, 1.0, 0.0)
        return carry

    lax.fori_loop(0, row_chunks, mark, 0)
    before = jnp.where(
        lax.broadcasted_iota(jnp.int32, (LANES, LANES), 0) < lax.broadcasted_iota(jnp.int32, (LANES, LANES), 1),
        1.0, 0.0).astype(jnp.bfloat16)
    excess = jnp.full((1, LANES), -1.0, jnp.float32)
    zero = jnp.zeros((1, LANES), jnp.float32)
    for r in range(2):
        local = jnp.dot(used[r].astype(jnp.bfloat16), before, preferred_element_type=jnp.float32)
        for c in range(row_chunks):
            if c % (row_chunks // 2) == 0:
                base = zero
            if c % (row_chunks // 4) == 0:
                run = zero
            flags = used[r, c:c + 1, :]
            if r == 0:
                rank = jnp.where(flags > 0.0, local[c:c + 1] + run, -1.0)
                at = slice(c * LANES, (c + 1) * LANES)
                ranks[0, :, at] = jnp.broadcast_to(jnp.where(flags > 0.0, rank + base, -1.0).astype(jnp.int32), (8, LANES))
                ranks[1, :, at] = jnp.broadcast_to(rank.astype(jnp.int32), (8, LANES))
            run = run + jnp.broadcast_to(jnp.sum(flags, axis=1, keepdims=True), (1, LANES))
            if (c + 1) % (row_chunks // 4) == 0:
                which = c // (row_chunks // 4)
                if r == 0:
                    counts[which] = jnp.broadcast_to(run.astype(jnp.int32), (8, LANES))
                if which in (0, 3):
                    excess = jnp.maximum(excess, run - float(room))
                base = base + run
                excess = jnp.maximum(excess, base - float(limit))
    unfit[0, 0] = jnp.max(excess).astype(jnp.int32)

    def one_hot(to, count, row):
        def some(n, carry):
            first = pl.multiple_of(n * 64, 64)
            at = first + lax.broadcasted_iota(jnp.int32, (64, row.shape[1]), 0)
            to[pl.ds(first, 64), :] = jnp.where(row == at, 1.0, 0.0).astype(jnp.bfloat16)
            return carry

        lax.fori_loop(0, count // 64, some, 0)

    own_rows = pl.ds(pl.multiple_of(z * tokens, tokens), tokens)

    @pl.when(outer)
    def _():
        one_hot(outer_pick, room, ranks[1, 0:1, own_rows])

    pass_on_from(edge)
    for k in range(1, 4):
        sums_to(k).wait()
    inverse = lax.rsqrt((sums[0] + sums[1] + sums[2] + sums[3]) / width + EPSILON)
    for tap in range(taps):
        invb[tap] = jnp.broadcast_to(inverse[tap:tap + 1, :], (LANES, tokens)).T
    gains.wait()

    def store(c):
        return pltpu.make_async_copy(pair.at[c, 0:tokens], united.at[c], osem.at[c])

    def rows_to(c):
        return pltpu.make_async_remote_copy(
            packed.at[c, 0:room], pair.at[c, tokens:tokens + room], nsend.at[c], nrecv.at[c],
            device_id=(g, near, t), device_id_type=MESH)

    def unite(c, carry):
        lanes = pl.ds(pl.multiple_of(c * LANES, LANES), LANES)
        scale = [gain[tap:tap + 1, lanes] for tap in range(taps)]
        for b in range(owned // step):
            total = jnp.zeros((step * block, LANES), jnp.float32)
            for tap in range(taps):
                x = xbuf[b * step:(b + 1) * step, tap, :, lanes].astype(jnp.float32).reshape(step * block, LANES)
                total = total + x * invb[tap, b * step * block:(b + 1) * step * block, :] * scale[tap]
            pair[c, b * step * block:(b + 1) * step * block, :] = total.astype(jnp.bfloat16)
        store(c).start()

        @pl.when(outer)
        def _():
            packed[c, 0:room, :] = jnp.dot(
                outer_pick[...], pair[c, 0:tokens, :], preferred_element_type=jnp.float32).astype(jnp.bfloat16)
            rows_to(c).start()

        return carry

    lax.fori_loop(0, 1, unite, 0)
    for i in (1, 2):
        @pl.when(z == 3 * i - 3)
        def _():
            heads_to(i, 1).start()

    lax.fori_loop(1, chunks // 2, unite, 0)
    pass_on_from(partner)
    lax.fori_loop(chunks // 2, chunks, unite, 0)
    pass_on_from(beyond)

    part = 2 * strip
    side = z - 1
    beside = t + 1 - 2 * lax.rem(t, 2)
    opposite = lax.rem(beside + 2, 4)

    def packed_to(c, which):
        here = packed.at[c, pl.ds(which * limit, limit)]
        return pltpu.make_async_remote_copy(
            here, here, psend.at[c], precv.at[c], device_id=(g, partner, t), device_id_type=MESH)

    def slots_to(row, piece, to, sem):
        here = slots.at[piece, pl.ds(row * strip, strip)]
        return pltpu.make_async_remote_copy(
            here, here, asend.at[sem + piece], arecv.at[sem + piece], device_id=(g, z, to), device_id_type=MESH)

    def back(c, piece, to):
        here = cbuf.at[c, piece]
        return pltpu.make_async_remote_copy(
            here, here, csend.at[piece, c], crecv.at[piece, c], device_id=(g, to, t), device_id_type=MESH)

    def back_whole(c, to):
        here = cbuf.at[c]
        return pltpu.make_async_remote_copy(
            here, here, csend.at[0, c], crecv.at[0, c], device_id=(g, to, t), device_id_type=MESH)

    @pl.when(inner)
    def _():
        outer_rank = lax.broadcasted_iota(jnp.int32, (1, room), 1)
        outer_count = jnp.concatenate([counts[edge, 0:1, :]] * (room // LANES), axis=1)
        outer_base = jnp.concatenate([jnp.where(z == 1, 0, counts[2, 0:1, :])] * (room // LANES), axis=1)
        one_hot(pair_pick, limit, jnp.concatenate([
            ranks[0, 0:1, own_rows], jnp.where(outer_rank < outer_count, outer_rank + outer_base, -1)], axis=1))

        def choose(n, carry):
            first = pl.multiple_of(n * 64, 64)
            at = first + lax.broadcasted_iota(jnp.int32, (64, tokens), 0)
            for k in range(4):
                chosen[pl.ds(first, 64), k * tokens:(k + 1) * tokens] = jnp.where(
                    places[k, 0:1, :] == at, 1.0, 0.0).astype(jnp.bfloat16)
            return carry


        def strip_of(piece, row):
            return piece, pl.ds(pl.multiple_of(row * strip, strip), strip)

        def heads_arrive(piece):
            for i in (1, 2):
                @pl.when(z == i)
                def _():
                    heads_own(i, piece).wait()
                    for k in range(4):
                        if piece == 0:
                            pass_on(here(k, 0), k).wait()
                        elif k != i:
                            heads_from(k, 1).wait_recv()

        def sum_first(n, carry):
            rows = pl.ds(pl.multiple_of(n * 384, 384), 384)
            some = jnp.dot(chosen[rows, :], given[:, strip:3 * strip], preferred_element_type=jnp.float32)
            some = some.T.astype(jnp.bfloat16)
            slots[(*strip_of(0, t), rows)] = some[0:strip]
            slots[(*strip_of(0, across), rows)] = some[strip:2 * strip]
            return carry

        def sum_second(n, carry):
            rows = pl.ds(pl.multiple_of(n * 384, 384), 384)
            some = jnp.dot(chosen[rows, :], given[:, 0:strip], preferred_element_type=jnp.float32)
            slots[(*strip_of(1, t), rows)] = some.T.astype(jnp.bfloat16)
            return carry

        def pack(c):
            rows_to(c).wait_recv()
            few = jnp.dot(pair_pick[...], pair[c], preferred_element_type=jnp.float32)
            packed[c, pl.ds(pl.multiple_of(side * limit, limit), limit), :] = few.astype(jnp.bfloat16)
            packed_to(c, side).start()

        mine = pl.multiple_of(jnp.where(z == 1, part, 0), part)
        theirs = pl.multiple_of(part - mine, part)

        def send_back(c, piece, go=True):
            cbuf[c, piece] = jnp.dot(
                slots[piece, pl.ds(theirs, part), :], packed[c], preferred_element_type=jnp.float32
            ).astype(jnp.bfloat16)
            if go:
                back(c, piece, edge).start()

        def keep(c):
            lanes = pl.ds(pl.multiple_of(c * LANES, LANES), LANES)
            for piece in range(2):
                rows = jnp.dot(
                    slots[piece, pl.ds(mine, part), :], packed[c], preferred_element_type=jnp.float32)
                for which in range(2):
                    first = which * part + piece * strip
                    out[first:first + strip, lanes] = rows[which * strip:(which + 1) * strip]

        def gathered(piece):
            if piece == 1:
                slots_to(across, piece, across, 0).wait_recv()
                slots_to(across, piece, beside, 4).start()
            slots_to(beside, piece, beside, 2).wait_recv()
            slots_to(opposite, piece, beside, 4).wait_recv()

        pack(0)
        lax.fori_loop(0, 2 * limit // 64, choose, 0)
        heads_arrive(0)
        lax.fori_loop(0, 2 * limit // 384, sum_first, 0)
        slots_to(t, 0, beside, 2).start()
        slots_to(across, 0, beside, 4).start()
        pack(1)
        heads_arrive(1)
        given_copy = pltpu.make_async_copy(given, given_out, dsem.at[0])
        given_copy.start()
        lax.fori_loop(0, 2 * limit // 384, sum_second, 0)
        slots_to(t, 1, across, 0).start()
        slots_to(t, 1, beside, 2).start()

        early, ahead = 1, 4
        pack(2)
        pack(3)
        gathered(0)
        for c in range(early):
            packed_to(c, 1 - side).wait_recv()
            send_back(c, 0)
            pack(c + ahead)
        gathered(1)
        for c in range(early):
            send_back(c, 1)

        def product(c, carry):
            packed_to(c, 1 - side).wait_recv()
            for piece in range(2):
                send_back(c, piece, False)
            back_whole(c, edge).start()

            @pl.when(c + ahead < chunks)
            def _():
                pack(c + ahead)

            keep(c - early)
            return carry

        lax.fori_loop(early, chunks, product, 0)

        def last(c, carry):
            keep(c)
            return carry

        lax.fori_loop(chunks - early, chunks, last, 0)

        def sent(c, carry):
            packed_to(c, side).wait_send()
            return carry

        lax.fori_loop(0, chunks, sent, 0)
        for c in range(early):
            for piece in range(2):
                back(c, piece, edge).wait_send()

        def sent_whole(c, carry):
            back_whole(c, edge).wait_send()
            return carry

        lax.fori_loop(early, chunks, sent_whole, 0)
        given_copy.wait()
        slots_to(t, 1, across, 0).wait_send()
        for piece in range(2):
            slots_to(t, piece, beside, 2).wait_send()
            slots_to(across, piece, beside, 4).wait_send()

    @pl.when(outer)
    def _():
        def place_rows(c, piece):
            lanes = pl.ds(pl.multiple_of(c * LANES, LANES), LANES)
            for which in range(2):
                first = which * part + piece * strip
                out[first:first + strip, lanes] = cbuf[c, piece, which * strip:(which + 1) * strip].astype(jnp.float32)

        for c in range(1):
            for piece in range(2):
                back(c, piece, near).wait_recv()
                place_rows(c, piece)

        def arrive(c, carry):
            back_whole(c, near).wait_recv()
            for piece in range(2):
                place_rows(c, piece)
            return carry

        lax.fori_loop(1, chunks, arrive, 0)

        def sent(c, carry):
            rows_to(c).wait_send()
            return carry

        lax.fori_loop(0, chunks, sent, 0)

    def stored(c, carry):
        store(c).wait()
        return carry

    lax.fori_loop(0, chunks, stored, 0)
    for i in (1, 2):
        @pl.when(z != i)
        def _():
            for piece in range(2):
                heads_to(i, piece).wait_send()
    for i in range(7):
        table_to(i).wait_send()


def whole_kernel(
    united, given, names, out,
    everywhere, slots, cbuf,
    lsem, usend, urecv, asend, arecv, csend, crecv,
):
    g, z, t = place()
    chunks, tokens, _ = united.shape
    strip = given.shape[1] // 3
    part = 2 * strip
    half = 2 * part
    inner = jnp.logical_or(z == 1, z == 2)
    outer = jnp.logical_not(inner)
    partner = 3 - z
    near = jnp.where(z < 2, 1, 2)
    far = 3 - near
    edge = jnp.where(z == 1, 0, 3)
    beyond = 3 - edge
    across = lax.rem(t + 2, 4)
    beside = t + 1 - 2 * lax.rem(t, 2)
    opposite = lax.rem(beside + 2, 4)
    barrier = pltpu.get_barrier_semaphore()

    def rows_to(c, to, sem):
        return pltpu.make_async_remote_copy(
            united.at[c], everywhere.at[c, pl.ds(z * tokens, tokens)], usend.at[sem, c], urecv.at[z, c],
            device_id=(g, to, t), device_id_type=MESH)

    def rows_from(c, k):
        return pltpu.make_async_remote_copy(
            united.at[c], everywhere.at[c, pl.ds(k * tokens, tokens)], usend.at[0, c], urecv.at[k, c],
            device_id=(g, partner, t), device_id_type=MESH)

    def slots_to(row, to, sem):
        here = slots.at[pl.ds(row * part, part)]
        return pltpu.make_async_remote_copy(
            here, here, asend.at[sem], arecv.at[sem], device_id=(g, z, to), device_id_type=MESH)

    def back(c, to):
        return pltpu.make_async_remote_copy(
            cbuf.at[c], cbuf.at[c], csend.at[c], crecv.at[c], device_id=(g, to, t), device_id_type=MESH)

    @pl.when(inner)
    def _():
        own = pltpu.make_async_copy(united, everywhere.at[:, pl.ds(z * tokens, tokens)], lsem.at[0])
        own.start()
        signal_all(barrier, [(g, partner, t), (g, edge, t), (g, beyond, t), (g, z, across), (g, z, beside)])
        pl.semaphore_wait(barrier, 5)

        def give(c, carry):
            rows_to(c, partner, 0).start()
            return carry

        lax.fori_loop(0, chunks, give, 0)

        def some_rows(j, carry):
            first = pl.multiple_of(j * 256, 256)
            total = sum_by_row(names, given, first, tokens).T.astype(jnp.bfloat16)
            for piece in range(2):
                slots[pl.ds(pl.multiple_of(t * part + piece * strip, strip), strip), pl.ds(first, 256)] = total[
                    (1 - piece) * strip:(2 - piece) * strip]
            return carry

        lax.fori_loop(0, 4 * tokens // 256, some_rows, 0)
        slots_to(t, across, 0).start()
        slots_to(t, beside, 1).start()
        own.wait()
        slots_to(across, across, 0).wait_recv()
        slots_to(across, beside, 2).start()
        slots_to(beside, beside, 1).wait_recv()
        slots_to(opposite, beside, 2).wait_recv()

        mine = pl.multiple_of(jnp.where(z == 1, half, 0), half)
        theirs = pl.multiple_of(half - mine, half)

        def product(c, carry):
            for k in range(4):
                @pl.when(z != k)
                def _():
                    rows_from(c, k).wait_recv()
            rows = everywhere[c]
            cbuf[c] = jnp.dot(
                slots[pl.ds(theirs, half), :], rows, preferred_element_type=jnp.float32).astype(jnp.bfloat16)
            back(c, edge).start()
            lanes = pl.ds(pl.multiple_of(c * LANES, LANES), LANES)
            out[:, lanes] = jnp.dot(
                slots[pl.ds(mine, half), :], rows, preferred_element_type=jnp.float32)
            return carry

        lax.fori_loop(0, chunks, product, 0)

        def sent(c, carry):
            rows_to(c, partner, 0).wait_send()
            back(c, edge).wait_send()
            return carry

        lax.fori_loop(0, chunks, sent, 0)
        slots_to(t, across, 0).wait_send()
        slots_to(t, beside, 1).wait_send()
        slots_to(across, beside, 2).wait_send()

    @pl.when(outer)
    def _():
        signal_all(barrier, [(g, near, t), (g, far, t)])
        pl.semaphore_wait(barrier, 2)

        def give(c, carry):
            rows_to(c, far, 0).start()
            rows_to(c, near, 1).start()
            return carry

        lax.fori_loop(0, chunks, give, 0)

        def arrive(c, carry):
            back(c, near).wait_recv()
            lanes = pl.ds(pl.multiple_of(c * LANES, LANES), LANES)
            out[:, lanes] = cbuf[c].astype(jnp.float32)
            return carry

        lax.fori_loop(0, chunks, arrive, 0)

        def sent(c, carry):
            rows_to(c, far, 0).wait_send()
            rows_to(c, near, 1).wait_send()
            return carry

        lax.fori_loop(0, chunks, sent, 0)


def line_body(feature_cache, owner_ids, slot_ids, live_tokens, tap_gain, key_cotangent, value_cotangent):
    owned, block, taps, columns = feature_cache.shape
    tokens = owned * block
    part = key_cotangent.shape[1]
    chunks = columns // LANES
    vmem, hbm = pl.BlockSpec(memory_space=pltpu.VMEM), pl.BlockSpec(memory_space=pltpu.HBM)
    dma = pltpu.SemaphoreType.DMA
    shape = jax.ShapeDtypeStruct

    def params(number, mebibytes):
        return pltpu.CompilerParams(
            collective_id=number, has_side_effects=True, vmem_limit_bytes=mebibytes * 2**20)

    room, limit = 3 * tokens // 4, 9 * tokens // 8
    shapes = (
        shape((2 * part, columns), jnp.float32),
        shape((chunks, tokens, LANES), jnp.bfloat16),
        shape((4 * tokens, part + part // 2), jnp.bfloat16),
        shape((4, 8, tokens), jnp.int32),
        shape((1, 1), jnp.int32),
    )
    gradient, united, given, names, unfit = pl.pallas_call(
        packed_kernel,
        out_shape=shapes,
        in_specs=[hbm] * 7,
        out_specs=(vmem, hbm, hbm, vmem, pl.BlockSpec(memory_space=pltpu.SMEM)),
        scratch_shapes=[
            pltpu.VMEM((4 * tokens, part + part // 2), jnp.bfloat16),
            pltpu.VMEM((owned, taps, block, columns), jnp.bfloat16),
            pltpu.VMEM((taps, columns), jnp.float32),
            pltpu.VMEM((3, 1, owned), jnp.int32),
            pltpu.VMEM((8, LANES), jnp.int32),
            pltpu.VMEM((8, 8, LANES), jnp.int32),
            pltpu.VMEM((8, 2, owned, LANES), jnp.float32),
            pltpu.VMEM((2, 4 * tokens // LANES, LANES), jnp.float32),
            pltpu.VMEM((2, 8, 4 * tokens), jnp.int32),
            pltpu.VMEM((4, 8, LANES), jnp.int32),
            pltpu.VMEM((taps, tokens, LANES), jnp.float32),
            pltpu.VMEM((4, 8, tokens), jnp.float32),
            pltpu.VMEM((taps, tokens, LANES), jnp.float32),
            pltpu.VMEM((chunks, tokens + room, LANES), jnp.bfloat16),
            pltpu.VMEM((2 * limit, 4 * tokens), jnp.bfloat16),
            pltpu.VMEM((limit, tokens + room), jnp.bfloat16),
            pltpu.VMEM((room, tokens), jnp.bfloat16),
            pltpu.VMEM((4, 8, tokens), jnp.int32),
            pltpu.VMEM((chunks, 2 * limit, LANES), jnp.bfloat16),
            pltpu.VMEM((2, 2 * part, 2 * limit), jnp.bfloat16),
            pltpu.VMEM((chunks, 2, part, LANES), jnp.bfloat16),
            dma((4,)), dma((4,)),
            dma((7,)), dma((8,)),
            dma((2, 2)), dma((2, 4)), dma((2,)),
            dma((4,)), dma((4,)),
            dma((3,)), dma((3,)),
            dma((chunks,)), dma((1,)),
            dma((chunks,)), dma((chunks,)),
            dma((chunks,)), dma((chunks,)),
            dma((6,)), dma((6,)),
            dma((2, chunks)), dma((2, chunks)),
        ],
        compiler_params=params(0, 58),
    )(
        jnp.transpose(feature_cache, (0, 2, 1, 3)), owner_ids.reshape(1, owned), slot_ids.reshape(1, owned),
        live_tokens.reshape(1, owned), tap_gain, key_cotangent, value_cotangent)

    def whole(_, *given):
        return pl.pallas_call(
            whole_kernel,
            out_shape=shapes[0],
            in_specs=[hbm, vmem, vmem],
            out_specs=vmem,
            scratch_shapes=[
                pltpu.VMEM((chunks, 4 * tokens, LANES), jnp.bfloat16),
                pltpu.VMEM((4 * part, 4 * tokens), jnp.bfloat16),
                pltpu.VMEM((chunks, 2 * part, LANES), jnp.bfloat16),
                dma((1,)),
                dma((2, chunks)), dma((4, chunks)),
                dma((3,)), dma((3,)),
                dma((chunks,)), dma((chunks,)),
            ],
            compiler_params=params(1, 40),
        )(*given)

    def fits(gradient, *_):
        return gradient

    return lax.cond(unfit[0, 0] <= 0, fits, whole, gradient, united, given, names)


def solution(mesh):
    in_specs = (
        P(("groups", "dp"), None, None, "tensor"),
        P(("groups", "dp"), None),
        P(("groups", "dp")),
        P(("groups", "dp")),
        P(None, "tensor"),
        P(("groups", "dp"), "tensor"),
        P(("groups", "dp"), "tensor"),
    )
    out_specs = P(("groups", "dp"), "tensor")
    line = tuple(mesh.shape[axis] for axis in ("groups", "dp", "tensor")) == (2, 4, 4)
    body = line_body if line else gather_body
    return jax.shard_map(body, mesh=mesh, in_specs=in_specs, out_specs=out_specs, check_vma=False)
```

```python
import functools

import jax
import jax.numpy as jnp
from jax import lax
from jax.experimental import pallas as pl
from jax.experimental.pallas import tpu as pltpu
from jax.sharding import PartitionSpec as P

EPSILON = 1e-06
MESH = pl.DeviceIdType.MESH
LANES = 128


def united_of(feature_cache, tap_gain, width):
    floats = feature_cache.astype(jnp.float32)
    squares = lax.psum(jnp.sum(floats * floats, axis=-1), "tensor")
    inverse_rms = lax.rsqrt(squares / width + EPSILON)
    return jnp.sum(floats * inverse_rms[..., None] * tap_gain, axis=2).astype(jnp.bfloat16)


def slot_matrix(owner_ids, slot_ids, live_tokens, owned, dtype):
    index = owner_ids[:, 0] * owned + slot_ids
    table = lax.all_gather(jnp.stack([index, live_tokens]), "dp", axis=1, tiled=True)
    slots = lax.axis_size("dp") * owned
    chosen = jnp.arange(slots, dtype=jnp.int32)[:, None] == table[0][None, :]
    return chosen.astype(dtype), table[1]


def gather_body(feature_cache, owner_ids, slot_ids, live_tokens, tap_gain, key_cotangent, value_cotangent):
    owned, block_len, _, columns = feature_cache.shape
    width = columns * lax.axis_size("tensor")
    united = united_of(feature_cache, tap_gain, width).reshape(owned * block_len, columns)
    everywhere = lax.all_gather(united, "dp", axis=0, tiled=True)
    chosen, live = slot_matrix(owner_ids, slot_ids, live_tokens, owned, jnp.bfloat16)
    joined = jnp.concatenate(
        [
            lax.all_gather(key_cotangent, "tensor", axis=1, tiled=True),
            lax.all_gather(value_cotangent, "tensor", axis=1, tiled=True),
        ],
        axis=1,
    )
    mine = lax.all_to_all(joined, "dp", split_axis=1, concat_axis=0, tiled=True)
    rows = mine.shape[1]
    mine = mine.reshape(-1, block_len, rows)
    mask = jnp.arange(block_len, dtype=jnp.int32)[None, :] < live[:, None]
    mine = jnp.where(mask[:, :, None], mine, jnp.zeros_like(mine)).reshape(-1, block_len * rows)
    by_slot = lax.dot_general(
        chosen, mine, (((1,), (0,)), ((), ())), preferred_element_type=jnp.float32
    ).astype(jnp.bfloat16).reshape(-1, rows)
    return lax.dot_general(
        by_slot, everywhere, (((0,), (0,)), ((), ())), preferred_element_type=jnp.float32
    )


def place():
    return tuple(lax.axis_index(n) for n in ("groups", "dp", "tensor"))


def signal_all(barrier, ids):
    for to in ids:
        pl.semaphore_signal(barrier, inc=1, device_id=to, device_id_type=MESH)


def sum_by_row(names, given, first, tokens):
    at = first + lax.broadcasted_iota(jnp.int32, (256, tokens), 0)
    total = jnp.zeros((256, given.shape[1]), jnp.float32)
    for k in range(4):
        chosen = jnp.where(names[k, 0:1, :] == at, 1.0, 0.0).astype(jnp.bfloat16)
        total = total + jnp.dot(chosen, given[k * tokens:(k + 1) * tokens, :], preferred_element_type=jnp.float32)
    return total


def packed_kernel(
    feats, owner, slot, live, gain_in, key, value,
    out, united, given_out, names, unfit,
    given, xbuf, gain, lists, table, tables, columns_of, used, ranks, counts, psq, sums, invb,
    pair, chosen, pair_pick, outer_pick, places, packed, slots, cbuf,
    xsem, lsem, bsend, brecv, gsend, grecv, hsem, fsend, frecv, ssend, srecv, osem, dsem,
    nsend, nrecv, psend, precv, asend, arecv, csend, crecv,
):
    g, z, t = place()
    owned, taps, block, columns = feats.shape
    tokens = owned * block
    chunks = columns // LANES
    width = columns * 4
    inner = jnp.logical_or(z == 1, z == 2)
    outer = jnp.logical_not(inner)
    room = outer_pick.shape[0]
    limit = pair_pick.shape[0]
    near = jnp.where(z < 2, 1, 2)
    fetches = 4
    per = owned // fetches

    def fetch(i):
        return pltpu.make_async_copy(feats.at[pl.ds(i * per, per)], xbuf.at[pl.ds(i * per, per)], xsem.at[i])

    small = [pltpu.make_async_copy(src, lists.at[i], lsem.at[i]) for i, src in enumerate((owner, slot, live))]
    for copy in small:
        copy.start()
    for i in range(fetches):
        fetch(i).start()
    gains = pltpu.make_async_copy(gain_in, gain, lsem.at[3])
    gains.start()

    barrier = pltpu.get_barrier_semaphore()
    others = [(g, lax.rem(z + k, 4), t) for k in range(1, 4)] + [(1 - g, lax.rem(z + k, 4), t) for k in range(4)]
    signal_all(barrier, others + [(g, z, lax.rem(t + k, 4)) for k in range(1, 4)])
    table[...] = jnp.zeros(table.shape, jnp.int32)
    for i, copy in enumerate(small):
        copy.wait()
        table[i:i + 1, 0:owned] = lists[i]
    pl.semaphore_wait(barrier, 10)

    def table_to(i):
        at = z if i < 3 else 4 + z
        return pltpu.make_async_remote_copy(
            table, tables.at[at], bsend.at[i], brecv.at[at], device_id=others[i], device_id_type=MESH)

    def table_from(at):
        return pltpu.make_async_remote_copy(
            table, tables.at[at], bsend.at[0], brecv.at[at], device_id=others[0], device_id_type=MESH)

    strip = key.shape[1] // 2
    across = lax.rem(t + 2, 4)
    edge = jnp.where(z == 1, 0, 3)
    partner, beyond = 3 - z, 3 - edge

    def heads(i, piece):
        return (key if i == 1 else value).at[:, piece * strip:(piece + 1) * strip]

    def here(k, piece):
        return given.at[pl.ds(k * tokens, tokens), (1 - piece) * strip:(2 - piece) * strip]

    def heads_to(i, piece):
        return pltpu.make_async_remote_copy(
            heads(i, piece), here(z, piece), gsend.at[piece, i - 1], grecv.at[piece, z],
            device_id=(g, i, t), device_id_type=MESH)

    def heads_from(k, piece):
        return pltpu.make_async_remote_copy(
            heads(1, piece), here(k, piece), gsend.at[piece, 0], grecv.at[piece, k],
            device_id=(g, near, t), device_id_type=MESH)

    def heads_own(i, piece):
        return pltpu.make_async_copy(heads(i, piece), here(i, piece), hsem.at[piece])

    def pass_on(src, k):
        return pltpu.make_async_remote_copy(
            src, given.at[pl.ds(k * tokens, tokens), 2 * strip:3 * strip], fsend.at[k], frecv.at[k],
            device_id=(g, z, across), device_id_type=MESH)

    def pass_on_from(k):
        @pl.when(inner)
        def _():
            heads_from(k, 0).wait_recv()
            pass_on(here(k, 0), k).start()

    for i in range(7):
        table_to(i).start()
    for i in (1, 2):
        @pl.when(z == i)
        def _():
            for piece in range(2):
                heads_to(3 - i, piece).start()
                heads_own(i, piece).start()
            pass_on(heads(i, 0), i).start()

        @pl.when(z == 6 - 3 * i)
        def _():
            heads_to(i, 0).start()
            heads_to(3 - i, 0).start()
            heads_to(i, 1).start()
    tables[z] = table[...]

    step = 8
    for i in range(fetches):
        fetch(i).wait()

        def squares(b, carry):
            first = pl.multiple_of(i * per + b * step, step)
            for tap in range(taps):
                total = jnp.zeros((step, block, LANES), jnp.float32)
                for c in range(chunks):
                    x = xbuf[pl.ds(first, step), tap, :, c * LANES:(c + 1) * LANES].astype(jnp.float32)
                    total = total + x * x
                psq[tap, pl.ds(pl.multiple_of(first * block, step * block), step * block), :] = total.reshape(
                    step * block, LANES)
            return carry

        lax.fori_loop(0, per // step, squares, 0)
    sums[0] = jnp.zeros((8, tokens), jnp.float32)
    for tap in range(taps):
        sums[0, tap:tap + 1, :] = jnp.sum(psq[tap].T, axis=0, keepdims=True)

    def sums_to(k):
        return pltpu.make_async_remote_copy(
            sums.at[0], sums.at[k], ssend.at[k - 1], srecv.at[k - 1],
            device_id=(g, z, lax.rem(t + k, 4)), device_id_type=MESH)

    for k in range(1, 4):
        sums_to(k).start()

    for k in range(1, 4):
        table_from(lax.rem(z + k, 4)).wait_recv()
    for k in range(4):
        table_from(4 + k).wait_recv()
    for k in range(8):
        index = (tables[k, 0:1, :] * owned + tables[k, 1:2, :]).astype(jnp.float32)
        columns_of[k, 0] = jnp.broadcast_to(index, (LANES, LANES)).T[0:owned]
        columns_of[k, 1] = jnp.broadcast_to(tables[k, 2:3, :].astype(jnp.float32), (LANES, LANES)).T[0:owned]

    def most_of(r, at):
        most = jnp.zeros((owned, LANES), jnp.float32)
        for k in range(4):
            most = jnp.maximum(most, jnp.where(columns_of[4 * r + k, 0] == at, columns_of[4 * r + k, 1], 0.0))
        return jnp.max(most, axis=0, keepdims=True)

    blocks = 4 * owned
    most = jnp.concatenate([
        most_of(0, (n * LANES + lax.broadcasted_iota(jnp.int32, (1, LANES), 1)).astype(jnp.float32))
        for n in range(blocks // LANES)], axis=1)
    most = jnp.broadcast_to(most, (8, blocks)).astype(jnp.bfloat16)
    token = lax.broadcasted_iota(jnp.int32, (LANES, tokens), 1)
    spread = jnp.where(
        lax.div(token, block) == lax.broadcasted_iota(jnp.int32, (LANES, tokens), 0), 1.0, 0.0).astype(jnp.bfloat16)
    offset = lax.rem(lax.broadcasted_iota(jnp.int32, (1, tokens), 1), block)
    for k in range(4):
        index = tables[k, 0:1, :] * owned + tables[k, 1:2, :]
        other = lax.broadcasted_iota(jnp.int32, (blocks, LANES), 0)
        ahead_of = jnp.where(
            jnp.logical_and(other < index, other >= jnp.where(index < blocks // 2, 0, blocks // 2)), 1.0, 0.0)
        rows_ahead = jnp.dot(most, ahead_of.astype(jnp.bfloat16), preferred_element_type=jnp.float32)[0:1].astype(jnp.int32)
        high = lax.div(rows_ahead, 64)
        entry = jnp.concatenate(
            [tables[k, 0:3, :], high, rows_ahead - 64 * high, jnp.zeros((3, LANES), jnp.int32)], axis=0)
        entry = jnp.dot(
            entry.astype(jnp.float32).astype(jnp.bfloat16), spread, preferred_element_type=jnp.float32
        ).astype(jnp.int32)
        alive = offset < entry[2:3]
        row = (entry[0:1] * owned + entry[1:2]) * block + offset
        names[k] = jnp.broadcast_to(jnp.where(alive, row, -1), (8, tokens))
        within = entry[3:4] * 64 + entry[4:5] + offset
        alive = jnp.logical_and(alive, within < limit)
        places[k] = jnp.broadcast_to(
            jnp.where(alive, within + jnp.where(entry[0:1] < 2, 0, limit), -1), (8, tokens))
    row_chunks = 4 * tokens // LANES

    def mark(c, carry):
        row = c * LANES + lax.broadcasted_iota(jnp.int32, (1, LANES), 1)
        at = lax.div(row, block).astype(jnp.float32)
        for r in range(2):
            most = most_of(r, at)
            used[r, pl.ds(c, 1), :] = jnp.where(lax.rem(row, block).astype(jnp.float32) < most, 1.0, 0.0)
        return carry

    lax.fori_loop(0, row_chunks, mark, 0)
    before = jnp.where(
        lax.broadcasted_iota(jnp.int32, (LANES, LANES), 0) < lax.broadcasted_iota(jnp.int32, (LANES, LANES), 1),
        1.0, 0.0).astype(jnp.bfloat16)
    excess = jnp.full((1, LANES), -1.0, jnp.float32)
    zero = jnp.zeros((1, LANES), jnp.float32)
    for r in range(2):
        local = jnp.dot(used[r].astype(jnp.bfloat16), before, preferred_element_type=jnp.float32)
        for c in range(row_chunks):
            if c % (row_chunks // 2) == 0:
                base = zero
            if c % (row_chunks // 4) == 0:
                run = zero
            flags = used[r, c:c + 1, :]
            if r == 0:
                rank = jnp.where(flags > 0.0, local[c:c + 1] + run, -1.0)
                at = slice(c * LANES, (c + 1) * LANES)
                ranks[0, :, at] = jnp.broadcast_to(jnp.where(flags > 0.0, rank + base, -1.0).astype(jnp.int32), (8, LANES))
                ranks[1, :, at] = jnp.broadcast_to(rank.astype(jnp.int32), (8, LANES))
            run = run + jnp.broadcast_to(jnp.sum(flags, axis=1, keepdims=True), (1, LANES))
            if (c + 1) % (row_chunks // 4) == 0:
                which = c // (row_chunks // 4)
                if r == 0:
                    counts[which] = jnp.broadcast_to(run.astype(jnp.int32), (8, LANES))
                if which in (0, 3):
                    excess = jnp.maximum(excess, run - float(room))
                base = base + run
                excess = jnp.maximum(excess, base - float(limit))
    unfit[0, 0] = jnp.max(excess).astype(jnp.int32)

    def one_hot(to, count, row):
        def some(n, carry):
            first = pl.multiple_of(n * 64, 64)
            at = first + lax.broadcasted_iota(jnp.int32, (64, row.shape[1]), 0)
            to[pl.ds(first, 64), :] = jnp.where(row == at, 1.0, 0.0).astype(jnp.bfloat16)
            return carry

        lax.fori_loop(0, count // 64, some, 0)

    own_rows = pl.ds(pl.multiple_of(z * tokens, tokens), tokens)

    @pl.when(outer)
    def _():
        one_hot(outer_pick, room, ranks[1, 0:1, own_rows])

    pass_on_from(edge)
    for k in range(1, 4):
        sums_to(k).wait()
    inverse = lax.rsqrt((sums[0] + sums[1] + sums[2] + sums[3]) / width + EPSILON)
    for tap in range(taps):
        invb[tap] = jnp.broadcast_to(inverse[tap:tap + 1, :], (LANES, tokens)).T
    gains.wait()

    def store(c):
        return pltpu.make_async_copy(pair.at[c, 0:tokens], united.at[c], osem.at[c])

    def rows_to(c):
        return pltpu.make_async_remote_copy(
            packed.at[c, 0:room], pair.at[c, tokens:tokens + room], nsend.at[c], nrecv.at[c],
            device_id=(g, near, t), device_id_type=MESH)

    def unite(c, carry):
        lanes = pl.ds(pl.multiple_of(c * LANES, LANES), LANES)
        scale = [gain[tap:tap + 1, lanes] for tap in range(taps)]
        for b in range(owned // step):
            total = jnp.zeros((step * block, LANES), jnp.float32)
            for tap in range(taps):
                x = xbuf[b * step:(b + 1) * step, tap, :, lanes].astype(jnp.float32).reshape(step * block, LANES)
                total = total + x * invb[tap, b * step * block:(b + 1) * step * block, :] * scale[tap]
            pair[c, b * step * block:(b + 1) * step * block, :] = total.astype(jnp.bfloat16)
        store(c).start()

        @pl.when(outer)
        def _():
            packed[c, 0:room, :] = jnp.dot(
                outer_pick[...], pair[c, 0:tokens, :], preferred_element_type=jnp.float32).astype(jnp.bfloat16)
            rows_to(c).start()

        return carry

    lax.fori_loop(0, 1, unite, 0)
    for i in (1, 2):
        @pl.when(z == 3 * i - 3)
        def _():
            heads_to(i, 1).start()

    lax.fori_loop(1, chunks // 2, unite, 0)
    pass_on_from(partner)
    lax.fori_loop(chunks // 2, chunks, unite, 0)
    pass_on_from(beyond)

    part = 2 * strip
    side = z - 1
    beside = t + 1 - 2 * lax.rem(t, 2)
    opposite = lax.rem(beside + 2, 4)

    def packed_to(c, which):
        here = packed.at[c, pl.ds(which * limit, limit)]
        return pltpu.make_async_remote_copy(
            here, here, psend.at[c], precv.at[c], device_id=(g, partner, t), device_id_type=MESH)

    def slots_to(row, piece, to, sem):
        here = slots.at[piece, pl.ds(row * strip, strip)]
        return pltpu.make_async_remote_copy(
            here, here, asend.at[sem + piece], arecv.at[sem + piece], device_id=(g, z, to), device_id_type=MESH)

    def back(c, piece, to):
        here = cbuf.at[c, piece]
        return pltpu.make_async_remote_copy(
            here, here, csend.at[piece, c], crecv.at[piece, c], device_id=(g, to, t), device_id_type=MESH)

    def back_whole(c, to):
        here = cbuf.at[c]
        return pltpu.make_async_remote_copy(
            here, here, csend.at[0, c], crecv.at[0, c], device_id=(g, to, t), device_id_type=MESH)

    @pl.when(inner)
    def _():
        outer_rank = lax.broadcasted_iota(jnp.int32, (1, room), 1)
        outer_count = jnp.concatenate([counts[edge, 0:1, :]] * (room // LANES), axis=1)
        outer_base = jnp.concatenate([jnp.where(z == 1, 0, counts[2, 0:1, :])] * (room // LANES), axis=1)
        one_hot(pair_pick, limit, jnp.concatenate([
            ranks[0, 0:1, own_rows], jnp.where(outer_rank < outer_count, outer_rank + outer_base, -1)], axis=1))

        def choose(n, carry):
            first = pl.multiple_of(n * 64, 64)
            at = first + lax.broadcasted_iota(jnp.int32, (64, tokens), 0)
            for k in range(4):
                chosen[pl.ds(first, 64), k * tokens:(k + 1) * tokens] = jnp.where(
                    places[k, 0:1, :] == at, 1.0, 0.0).astype(jnp.bfloat16)
            return carry


        def strip_of(piece, row):
            return piece, pl.ds(pl.multiple_of(row * strip, strip), strip)

        def heads_arrive(piece):
            for i in (1, 2):
                @pl.when(z == i)
                def _():
                    heads_own(i, piece).wait()
                    for k in range(4):
                        if piece == 0:
                            pass_on(here(k, 0), k).wait()
                        elif k != i:
                            heads_from(k, 1).wait_recv()

        def sum_first(n, carry):
            rows = pl.ds(pl.multiple_of(n * 384, 384), 384)
            some = jnp.dot(chosen[rows, :], given[:, strip:3 * strip], preferred_element_type=jnp.float32)
            some = some.T.astype(jnp.bfloat16)
            slots[(*strip_of(0, t), rows)] = some[0:strip]
            slots[(*strip_of(0, across), rows)] = some[strip:2 * strip]
            return carry

        def sum_second(n, carry):
            rows = pl.ds(pl.multiple_of(n * 384, 384), 384)
            some = jnp.dot(chosen[rows, :], given[:, 0:strip], preferred_element_type=jnp.float32)
            slots[(*strip_of(1, t), rows)] = some.T.astype(jnp.bfloat16)
            return carry

        def pack(c):
            rows_to(c).wait_recv()
            few = jnp.dot(pair_pick[...], pair[c], preferred_element_type=jnp.float32)
            packed[c, pl.ds(pl.multiple_of(side * limit, limit), limit), :] = few.astype(jnp.bfloat16)
            packed_to(c, side).start()

        mine = pl.multiple_of(jnp.where(z == 1, part, 0), part)
        theirs = pl.multiple_of(part - mine, part)

        def send_back(c, piece):
            cbuf[c, piece] = jnp.dot(
                slots[piece, pl.ds(theirs, part), :], packed[c], preferred_element_type=jnp.float32
            ).astype(jnp.bfloat16)
            back(c, piece, edge).start()

        def keep(c):
            lanes = pl.ds(pl.multiple_of(c * LANES, LANES), LANES)
            for piece in range(2):
                rows = jnp.dot(
                    slots[piece, pl.ds(mine, part), :], packed[c], preferred_element_type=jnp.float32)
                for which in range(2):
                    first = which * part + piece * strip
                    out[first:first + strip, lanes] = rows[which * strip:(which + 1) * strip]

        def gathered(piece):
            if piece == 1:
                slots_to(across, piece, across, 0).wait_recv()
                slots_to(across, piece, beside, 4).start()
            slots_to(beside, piece, beside, 2).wait_recv()
            slots_to(opposite, piece, beside, 4).wait_recv()

        pack(0)
        lax.fori_loop(0, 2 * limit // 64, choose, 0)
        heads_arrive(0)
        lax.fori_loop(0, 2 * limit // 384, sum_first, 0)
        slots_to(t, 0, beside, 2).start()
        slots_to(across, 0, beside, 4).start()
        pack(1)
        heads_arrive(1)
        given_copy = pltpu.make_async_copy(given, given_out, dsem.at[0])
        given_copy.start()
        lax.fori_loop(0, 2 * limit // 384, sum_second, 0)
        slots_to(t, 1, across, 0).start()
        slots_to(t, 1, beside, 2).start()

        early, ahead = 1, 4
        pack(2)
        pack(3)
        gathered(0)
        for c in range(early):
            packed_to(c, 1 - side).wait_recv()
            send_back(c, 0)
            pack(c + ahead)
        gathered(1)
        for c in range(early):
            send_back(c, 1)

        def product(c, carry):
            packed_to(c, 1 - side).wait_recv()
            both = slots[:, pl.ds(theirs, part), :].reshape(2 * part, 2 * limit)
            cbuf[c] = jnp.dot(both, packed[c], preferred_element_type=jnp.float32).astype(jnp.bfloat16).reshape(
                2, part, LANES)
            back_whole(c, edge).start()

            @pl.when(c + ahead < chunks)
            def _():
                pack(c + ahead)

            keep(c - early)
            return carry

        lax.fori_loop(early, chunks, product, 0)

        def last(c, carry):
            keep(c)
            return carry

        lax.fori_loop(chunks - early, chunks, last, 0)

        def sent(c, carry):
            packed_to(c, side).wait_send()
            return carry

        lax.fori_loop(0, chunks, sent, 0)
        for c in range(early):
            for piece in range(2):
                back(c, piece, edge).wait_send()

        def sent_whole(c, carry):
            back_whole(c, edge).wait_send()
            return carry

        lax.fori_loop(early, chunks, sent_whole, 0)
        given_copy.wait()
        slots_to(t, 1, across, 0).wait_send()
        for piece in range(2):
            slots_to(t, piece, beside, 2).wait_send()
            slots_to(across, piece, beside, 4).wait_send()

    @pl.when(outer)
    def _():
        def place_rows(c, piece):
            lanes = pl.ds(pl.multiple_of(c * LANES, LANES), LANES)
            for which in range(2):
                first = which * part + piece * strip
                out[first:first + strip, lanes] = cbuf[c, piece, which * strip:(which + 1) * strip].astype(jnp.float32)

        for c in range(1):
            for piece in range(2):
                back(c, piece, near).wait_recv()
                place_rows(c, piece)

        def arrive(c, carry):
            back_whole(c, near).wait_recv()
            for piece in range(2):
                place_rows(c, piece)
            return carry

        lax.fori_loop(1, chunks, arrive, 0)

        def sent(c, carry):
            rows_to(c).wait_send()
            return carry

        lax.fori_loop(0, chunks, sent, 0)

    def stored(c, carry):
        store(c).wait()
        return carry

    lax.fori_loop(0, chunks, stored, 0)
    for i in (1, 2):
        @pl.when(z != i)
        def _():
            for piece in range(2):
                heads_to(i, piece).wait_send()
    for i in range(7):
        table_to(i).wait_send()


def whole_kernel(
    united, given, names, out,
    everywhere, slots, cbuf,
    lsem, usend, urecv, asend, arecv, csend, crecv,
):
    g, z, t = place()
    chunks, tokens, _ = united.shape
    strip = given.shape[1] // 3
    part = 2 * strip
    half = 2 * part
    inner = jnp.logical_or(z == 1, z == 2)
    outer = jnp.logical_not(inner)
    partner = 3 - z
    near = jnp.where(z < 2, 1, 2)
    far = 3 - near
    edge = jnp.where(z == 1, 0, 3)
    beyond = 3 - edge
    across = lax.rem(t + 2, 4)
    beside = t + 1 - 2 * lax.rem(t, 2)
    opposite = lax.rem(beside + 2, 4)
    barrier = pltpu.get_barrier_semaphore()

    def rows_to(c, to, sem):
        return pltpu.make_async_remote_copy(
            united.at[c], everywhere.at[c, pl.ds(z * tokens, tokens)], usend.at[sem, c], urecv.at[z, c],
            device_id=(g, to, t), device_id_type=MESH)

    def rows_from(c, k):
        return pltpu.make_async_remote_copy(
            united.at[c], everywhere.at[c, pl.ds(k * tokens, tokens)], usend.at[0, c], urecv.at[k, c],
            device_id=(g, partner, t), device_id_type=MESH)

    def slots_to(row, to, sem):
        here = slots.at[pl.ds(row * part, part)]
        return pltpu.make_async_remote_copy(
            here, here, asend.at[sem], arecv.at[sem], device_id=(g, z, to), device_id_type=MESH)

    def back(c, to):
        return pltpu.make_async_remote_copy(
            cbuf.at[c], cbuf.at[c], csend.at[c], crecv.at[c], device_id=(g, to, t), device_id_type=MESH)

    @pl.when(inner)
    def _():
        own = pltpu.make_async_copy(united, everywhere.at[:, pl.ds(z * tokens, tokens)], lsem.at[0])
        own.start()
        signal_all(barrier, [(g, partner, t), (g, edge, t), (g, beyond, t), (g, z, across), (g, z, beside)])
        pl.semaphore_wait(barrier, 5)

        def give(c, carry):
            rows_to(c, partner, 0).start()
            return carry

        lax.fori_loop(0, chunks, give, 0)

        def some_rows(j, carry):
            first = pl.multiple_of(j * 256, 256)
            total = sum_by_row(names, given, first, tokens).T.astype(jnp.bfloat16)
            for piece in range(2):
                slots[pl.ds(pl.multiple_of(t * part + piece * strip, strip), strip), pl.ds(first, 256)] = total[
                    (1 - piece) * strip:(2 - piece) * strip]
            return carry

        lax.fori_loop(0, 4 * tokens // 256, some_rows, 0)
        slots_to(t, across, 0).start()
        slots_to(t, beside, 1).start()
        own.wait()
        slots_to(across, across, 0).wait_recv()
        slots_to(across, beside, 2).start()
        slots_to(beside, beside, 1).wait_recv()
        slots_to(opposite, beside, 2).wait_recv()

        mine = pl.multiple_of(jnp.where(z == 1, half, 0), half)
        theirs = pl.multiple_of(half - mine, half)

        def product(c, carry):
            for k in range(4):
                @pl.when(z != k)
                def _():
                    rows_from(c, k).wait_recv()
            rows = everywhere[c]
            cbuf[c] = jnp.dot(
                slots[pl.ds(theirs, half), :], rows, preferred_element_type=jnp.float32).astype(jnp.bfloat16)
            back(c, edge).start()
            lanes = pl.ds(pl.multiple_of(c * LANES, LANES), LANES)
            out[:, lanes] = jnp.dot(
                slots[pl.ds(mine, half), :], rows, preferred_element_type=jnp.float32)
            return carry

        lax.fori_loop(0, chunks, product, 0)

        def sent(c, carry):
            rows_to(c, partner, 0).wait_send()
            back(c, edge).wait_send()
            return carry

        lax.fori_loop(0, chunks, sent, 0)
        slots_to(t, across, 0).wait_send()
        slots_to(t, beside, 1).wait_send()
        slots_to(across, beside, 2).wait_send()

    @pl.when(outer)
    def _():
        signal_all(barrier, [(g, near, t), (g, far, t)])
        pl.semaphore_wait(barrier, 2)

        def give(c, carry):
            rows_to(c, far, 0).start()
            rows_to(c, near, 1).start()
            return carry

        lax.fori_loop(0, chunks, give, 0)

        def arrive(c, carry):
            back(c, near).wait_recv()
            lanes = pl.ds(pl.multiple_of(c * LANES, LANES), LANES)
            out[:, lanes] = cbuf[c].astype(jnp.float32)
            return carry

        lax.fori_loop(0, chunks, arrive, 0)

        def sent(c, carry):
            rows_to(c, far, 0).wait_send()
            rows_to(c, near, 1).wait_send()
            return carry

        lax.fori_loop(0, chunks, sent, 0)


def line_body(feature_cache, owner_ids, slot_ids, live_tokens, tap_gain, key_cotangent, value_cotangent):
    owned, block, taps, columns = feature_cache.shape
    tokens = owned * block
    part = key_cotangent.shape[1]
    chunks = columns // LANES
    vmem, hbm = pl.BlockSpec(memory_space=pltpu.VMEM), pl.BlockSpec(memory_space=pltpu.HBM)
    dma = pltpu.SemaphoreType.DMA
    shape = jax.ShapeDtypeStruct

    def params(number, mebibytes):
        return pltpu.CompilerParams(
            collective_id=number, has_side_effects=True, vmem_limit_bytes=mebibytes * 2**20)

    room, limit = 3 * tokens // 4, 9 * tokens // 8
    shapes = (
        shape((2 * part, columns), jnp.float32),
        shape((chunks, tokens, LANES), jnp.bfloat16),
        shape((4 * tokens, part + part // 2), jnp.bfloat16),
        shape((4, 8, tokens), jnp.int32),
        shape((1, 1), jnp.int32),
    )
    gradient, united, given, names, unfit = pl.pallas_call(
        packed_kernel,
        out_shape=shapes,
        in_specs=[hbm] * 7,
        out_specs=(vmem, hbm, hbm, vmem, pl.BlockSpec(memory_space=pltpu.SMEM)),
        scratch_shapes=[
            pltpu.VMEM((4 * tokens, part + part // 2), jnp.bfloat16),
            pltpu.VMEM((owned, taps, block, columns), jnp.bfloat16),
            pltpu.VMEM((taps, columns), jnp.float32),
            pltpu.VMEM((3, 1, owned), jnp.int32),
            pltpu.VMEM((8, LANES), jnp.int32),
            pltpu.VMEM((8, 8, LANES), jnp.int32),
            pltpu.VMEM((8, 2, owned, LANES), jnp.float32),
            pltpu.VMEM((2, 4 * tokens // LANES, LANES), jnp.float32),
            pltpu.VMEM((2, 8, 4 * tokens), jnp.int32),
            pltpu.VMEM((4, 8, LANES), jnp.int32),
            pltpu.VMEM((taps, tokens, LANES), jnp.float32),
            pltpu.VMEM((4, 8, tokens), jnp.float32),
            pltpu.VMEM((taps, tokens, LANES), jnp.float32),
            pltpu.VMEM((chunks, tokens + room, LANES), jnp.bfloat16),
            pltpu.VMEM((2 * limit, 4 * tokens), jnp.bfloat16),
            pltpu.VMEM((limit, tokens + room), jnp.bfloat16),
            pltpu.VMEM((room, tokens), jnp.bfloat16),
            pltpu.VMEM((4, 8, tokens), jnp.int32),
            pltpu.VMEM((chunks, 2 * limit, LANES), jnp.bfloat16),
            pltpu.VMEM((2, 2 * part, 2 * limit), jnp.bfloat16),
            pltpu.VMEM((chunks, 2, part, LANES), jnp.bfloat16),
            dma((4,)), dma((4,)),
            dma((7,)), dma((8,)),
            dma((2, 2)), dma((2, 4)), dma((2,)),
            dma((4,)), dma((4,)),
            dma((3,)), dma((3,)),
            dma((chunks,)), dma((1,)),
            dma((chunks,)), dma((chunks,)),
            dma((chunks,)), dma((chunks,)),
            dma((6,)), dma((6,)),
            dma((2, chunks)), dma((2, chunks)),
        ],
        compiler_params=params(0, 58),
    )(
        jnp.transpose(feature_cache, (0, 2, 1, 3)), owner_ids.reshape(1, owned), slot_ids.reshape(1, owned),
        live_tokens.reshape(1, owned), tap_gain, key_cotangent, value_cotangent)

    def whole(_, *given):
        return pl.pallas_call(
            whole_kernel,
            out_shape=shapes[0],
            in_specs=[hbm, vmem, vmem],
            out_specs=vmem,
            scratch_shapes=[
                pltpu.VMEM((chunks, 4 * tokens, LANES), jnp.bfloat16),
                pltpu.VMEM((4 * part, 4 * tokens), jnp.bfloat16),
                pltpu.VMEM((chunks, 2 * part, LANES), jnp.bfloat16),
                dma((1,)),
                dma((2, chunks)), dma((4, chunks)),
                dma((3,)), dma((3,)),
                dma((chunks,)), dma((chunks,)),
            ],
            compiler_params=params(1, 40),
        )(*given)

    def fits(gradient, *_):
        return gradient

    return lax.cond(unfit[0, 0] <= 0, fits, whole, gradient, united, given, names)


def solution(mesh):
    in_specs = (
        P(("groups", "dp"), None, None, "tensor"),
        P(("groups", "dp"), None),
        P(("groups", "dp")),
        P(("groups", "dp")),
        P(None, "tensor"),
        P(("groups", "dp"), "tensor"),
        P(("groups", "dp"), "tensor"),
    )
    out_specs = P(("groups", "dp"), "tensor")
    line = tuple(mesh.shape[axis] for axis in ("groups", "dp", "tensor")) == (2, 4, 4)
    body = line_body if line else gather_body
    return jax.shard_map(body, mesh=mesh, in_specs=in_specs, out_specs=out_specs, check_vma=False)
```
